32 devices in a mesh: dp: 2 (over x), ep: 16 (over z, y, core).
Axes of the slice: x: 2, y: 2, z: 4, core: 2. Of those that a mesh axis runs over, the one named last changes fastest.
Arguments:
- tokens: bfloat16 [8192, 512], P(('dp', 'ep')), parts along dimension 0, may hold values from -6 to 6
- routes: int32 [8192, 2], P(('dp', 'ep')), parts along dimension 0, may hold values from 0 to 15, all different within a row; in each aligned block of 256 rows (0 to 255, 256 to 511, ...) at most 64 rows name the same one
- capacity: int32 [16], replicated, may hold values from 32 to 64, as said below
- expert_in: bfloat16 [16, 512, 2048], P('ep'), may hold values from -0.25 to 0.25
- expert_out: bfloat16 [16, 2048, 512], P('ep'), may hold values from -0.125 to 0.125
- shared_in: bfloat16 [2, 2048, 512], P(None, 'ep'), may hold values from -0.25 to 0.25
- shared_out: bfloat16 [2, 2048, 512], P(None, 'ep'), may hold values from -0.125 to 0.125
- route_gate: bfloat16 [16, 6144], P('ep'), may hold values from -0.25 to 0.25
- shared_gate: bfloat16 [2, 6144], replicated, may hold values from -0.25 to 0.25
Outputs:
- mixed: bfloat16 [8192, 12, 512], P(('dp', 'ep')), parts along dimension 0
The draws below stay inside these ranges and needn't reach their ends.
There are 2 independent parts, one for each index of `dp`. The reference program is written for one: setup_inputs(seed, part) draws one part's arguments, and reference() takes and returns one part's arrays. A program takes and returns all parts, laid end to end along the dimension named above; an argument that names none is the same for every part. Nothing has to cross between parts.
Inputs may be any that keep to these rules, and one draw needn't show every extreme that they name: `routes`: each sample names 2 different experts. Within each device's block of 256 samples no expert is named more than 64 times. `capacity`: some expert accepts exactly 64 rows.
All inputs are finite; a program needn't handle non-finite values.
Results may differ from the reference program's by a relative error of at most 0.0054.
Values may be sent and summed in bfloat16 or wider, within the bound.
No kernel may reach another device: no remote copies, remote signals or barrier semaphores. Data moves between devices by JAX's collectives and lax.ppermute only.
A program may use at most 64 MiB of HBM per device.

```python
import math
import jax
import jax.numpy as jnp
import numpy as np
from jax import lax

D = 512
H = 2048
TASKS = 12
SHARED = 2
TOP = 2
TOK_DEV = 256
EXPERTS = 16
CAP = 64
TOKENS = 4096
N_EP = 16


def draw_capacity(key, part):
    first = jax.random.fold_in(key, 11)
    second = jax.random.fold_in(key, 23)
    lowest = max(2, CAP // 2)
    values = jax.random.randint(first, (EXPERTS,), lowest, CAP + 1)
    chosen = jax.random.randint(second, (), 0, EXPERTS)
    return jnp.where(jnp.arange(EXPERTS) == chosen, CAP, values).astype(jnp.int32)


def steps_of(key, extent, pieces, low, high):
    def one(dim, blocks):
        steps = jax.random.uniform(jax.random.fold_in(jax.random.fold_in(key, 6), dim), (blocks,), jnp.float32, low / len(pieces), high / len(pieces))
        return jnp.repeat(jnp.exp(steps), extent[dim] // blocks).reshape((-1,) + (1,) * (len(extent) - dim - 1))

    level = one(*pieces[0])
    for cut in pieces[1:]:
        level = level * one(*cut)
    return level


def deal_out(stream_key, own, number, rows, number_of, top, limit, slope):
    sequence = jax.random.permutation(stream_key, number_of)
    crowded, usual = portions_of(number_of, rows * top, limit, slope, True), portions_of(number_of, rows * top, limit, slope, False)
    places = jnp.arange(number_of)

    def named(tallies, offset_by):
        used = int((tallies > 0).sum())
        fixed = max(1, used // 4)
        passed = fixed + (places - fixed + offset_by * (used - fixed)) % max(1, number_of - fixed)
        return jnp.zeros((number_of,), jnp.int32).at[sequence[jnp.where(places < fixed, places, passed)]].set(jnp.asarray(tallies, jnp.int32))

    tallies = jnp.where(number % 4 == 0, named(crowded, number // 4), named(usual, number - number // 4 - 1))
    mixed = jax.random.permutation(jax.random.fold_in(own, 3), number_of)
    donor, sink = mixed[0:number_of // 2 * 2:2], mixed[1:number_of // 2 * 2:2]
    slack = jnp.minimum(tallies[donor] - 1, limit - tallies[sink]) // 2
    slack = jnp.where((donor == sequence[0]) | (sink == sequence[0]) | (tallies[sink] == 0), 0, jnp.maximum(slack, 0))
    passed = jax.random.randint(jax.random.fold_in(own, 4), (number_of // 2,), 0, 1 << 20) % (slack + 1)
    tallies = tallies.at[donor].add(-passed).at[sink].add(passed)
    members = jnp.searchsorted(jnp.cumsum(tallies), jnp.arange(rows * top), side="right").astype(jnp.int32)
    listing = members.reshape(top, rows).T
    listing = listing[jax.random.permutation(jax.random.fold_in(own, 1), rows)]
    offset_by = jax.random.randint(jax.random.fold_in(own, 2), (rows, 1), 0, top)
    return jnp.take_along_axis(listing, (jnp.arange(top)[None, :] + offset_by) % top, axis=1)


def portions_of(count, total, bound, skew, full):
    weights = [(1 << 20) // math.isqrt(rank ** skew) + 1 for rank in range(1, count + 1)]
    largest = bound if full else min(bound, max(-(-total // count), total * weights[0] // sum(weights)))
    least = 1 if total - largest >= count - 1 else 0
    holding, spare = [largest] + [least] * (count - 1), total - largest - least * (count - 1)
    while spare > 0:
        free = [i for i in range(1, count) if holding[i] < largest] or [i for i in range(1, count) if holding[i] < bound]
        pool, remaining = sum([weights[i] for i in free]), spare
        for i in free:
            more = min(bound - holding[i], max(1, remaining * weights[i] // pool), spare)
            holding[i] = holding[i] + more
            spare = spare - more
    return np.array(holding)


def centred(own_key, shape, width, reach, split=(), kind=jnp.bfloat16):
    gain = steps_of(own_key, shape, split, -0.22, 0.18) if split else 1.0
    entries = jax.random.normal(own_key, shape, jnp.float32) * width * gain
    return jnp.minimum(jnp.maximum(entries, -reach), reach).astype(kind)


def setup_inputs(seed: int = 0, part: int = 0) -> dict:
    keys = jax.random.split(jax.random.key(seed), 10)
    own_keys = jax.random.split(jax.random.fold_in(keys[9], part), 10)
    tokens = centred(own_keys[0], (TOKENS, D), 1.0, 6.0, ((0, 16),))
    routes_keys = jax.random.split(jax.random.fold_in(own_keys[1], 1), TOKENS // TOK_DEV)
    routes_turns = jax.random.permutation(jax.random.fold_in(own_keys[1], 3), TOKENS // TOK_DEV)
    routes = jax.vmap(lambda own, number: deal_out(jax.random.fold_in(own_keys[1], 2), own, number, TOK_DEV, EXPERTS, TOP, CAP, 2))(routes_keys, routes_turns).reshape((TOKENS, TOP))
    capacity = draw_capacity(jax.random.fold_in(keys[9], 71), part)
    expert_in = centred(keys[3], (EXPERTS, D, H), D ** -0.5, 0.25, ((0, 16),))
    expert_out = centred(keys[4], (EXPERTS, H, D), H ** -0.5, 0.125, ((0, 16),))
    shared_in = centred(keys[5], (SHARED, H, D), D ** -0.5, 0.25, ((1, 16),))
    shared_out = centred(keys[6], (SHARED, H, D), H ** -0.5, 0.125, ((1, 16),))
    route_gate = centred(keys[7], (EXPERTS, TASKS * D), D ** -0.5, 0.25, ((0, 16),))
    shared_gate = centred(keys[8], (SHARED, TASKS * D), D ** -0.5, 0.25)
    return dict(tokens=tokens, routes=routes, capacity=capacity, expert_in=expert_in, expert_out=expert_out, shared_in=shared_in, shared_out=shared_out, route_gate=route_gate, shared_gate=shared_gate)


def slot_ranks(routes, capacity):
    blocks = routes.reshape(N_EP, -1)
    chosen = (blocks[:, :, None] == jnp.arange(EXPERTS, dtype=jnp.int32)[None, None, :]).astype(jnp.int32)
    ranked = jnp.sum((jnp.cumsum(chosen, axis=1) - chosen) * chosen, axis=2)
    kept = ranked < capacity[blocks]
    return blocks, ranked.astype(jnp.int32), kept


def reference(tokens, routes, capacity, expert_in, expert_out, shared_in, shared_out, route_gate, shared_gate):
    blocks, ranked, kept = slot_ranks(routes, capacity)
    count = blocks.shape[1]
    owner = jnp.arange(N_EP, dtype=jnp.int32)[:, None]
    position = owner * CAP + ranked
    token_index = owner * TOK_DEV + jnp.arange(count, dtype=jnp.int32)[None, :] // TOP
    flat_slot = blocks * (N_EP * CAP) + position
    target = jnp.where(kept, flat_slot, EXPERTS * N_EP * CAP).reshape(-1)
    source = jnp.full((EXPERTS * N_EP * CAP,), -1, jnp.int32)
    source = source.at[target].set(token_index.reshape(-1), mode="drop").reshape(EXPERTS, N_EP * CAP)

    def serve(item):
        index, w_in, w_out, gate_row = item
        rows = jnp.where(index[:, None] >= 0, tokens[jnp.maximum(index, 0)], jnp.zeros((), tokens.dtype))
        hidden = jax.nn.gelu(jnp.dot(rows, w_in, preferred_element_type=jnp.float32)).astype(jnp.bfloat16)
        out_rows = jnp.dot(hidden, w_out, preferred_element_type=jnp.float32).astype(jnp.bfloat16)
        scores = lax.dot_general(rows, gate_row.reshape(TASKS, D), (((1,), (1,)), ((), ())),
                                 preferred_element_type=jnp.float32).astype(jnp.bfloat16)
        return out_rows, scores

    served, scored = lax.map(serve, (source, expert_in, expert_out, route_gate))
    pick = flat_slot.reshape(-1)
    pair_rows = served.reshape(-1, D)[pick].reshape(N_EP, TOK_DEV, TOP, D)
    pair_scores = scored.reshape(-1, TASKS)[pick].reshape(N_EP, TOK_DEV, TOP, TASKS)
    keep = kept.reshape(N_EP, TOK_DEV, TOP)
    up_full = shared_in.astype(jnp.float32)
    down_full = shared_out.astype(jnp.float32)
    gate_full = shared_gate.reshape(SHARED * TASKS, D)

    def finish(item):
        block, prow, pscore, keep_block = item
        hidden = jax.nn.gelu(jnp.einsum("td,shd->sth", block.astype(jnp.float32), up_full)).astype(jnp.bfloat16)
        shared_rows = jnp.einsum("sth,shd->std", hidden.astype(jnp.float32), down_full)
        shared_logits = lax.dot_general(block, gate_full, (((1,), (1,)), ((), ())),
                                        preferred_element_type=jnp.float32).astype(jnp.bfloat16)
        shared_values = jax.nn.sigmoid(shared_logits.astype(jnp.float32)).reshape(TOK_DEV, SHARED, TASKS)
        routed_values = keep_block.astype(jnp.float32)[:, :, None] * jax.nn.sigmoid(pscore.astype(jnp.float32))
        total = jnp.sum(routed_values, axis=1) + jnp.sum(shared_values, axis=1)
        mixed = jnp.zeros((TOK_DEV, TASKS, D), jnp.float32)
        for k in range(TOP):
            mixed = mixed + (routed_values[:, k] / total)[:, :, None] * prow[:, k].astype(jnp.float32)[:, None, :]
        for s in range(SHARED):
            mixed = mixed + (shared_values[:, s] / total)[:, :, None] * shared_rows[s][:, None, :]
        return mixed.astype(jnp.bfloat16)

    result = lax.map(finish, (tokens.reshape(N_EP, TOK_DEV, D), pair_rows, pair_scores, keep))
    return result.reshape(TOKENS, TASKS, D)
```

```python
import functools

import jax
import jax.numpy as jnp
from jax import lax
from jax.experimental import pallas as pl
from jax.experimental.pallas import tpu as pltpu
from jax.sharding import PartitionSpec as P

BF, F32, I32 = jnp.bfloat16, jnp.float32, jnp.int32
PAD = 16


def whole(shape):
    return pl.BlockSpec(shape, lambda *_: (0,) * len(shape))


def call(kernel, out_shape, **kw):
    return pl.pallas_call(kernel, out_shape=out_shape, **kw)


def cost(flops, size):
    return pl.CostEstimate(flops=int(flops), bytes_accessed=int(size), transcendentals=0)


def dot_t(a, b):
    return lax.dot_general(a, b, (((1,), (1,)), ((), ())), preferred_element_type=F32)


def pack_kernel(tasks, pick_ref, in_ref, out_ref, gate_ref, packed_ref):
    units, width = in_ref.shape[1:]
    packed_ref[0:units] = in_ref[0]
    packed_ref[units : 2 * units] = out_ref[0]
    packed_ref[2 * units :] = jnp.zeros((packed_ref.shape[0] - 2 * units, width), BF)
    for s in range(tasks):
        row = 2 * units + s
        packed_ref[row : row + 1] = gate_ref[:, s * width : (s + 1) * width]


def pack(pick, shared_in, shared_out, route_gate, tasks):
    _, units, width = shared_in.shape
    rows = 2 * units + -(-tasks // PAD) * PAD
    block = pl.BlockSpec((1, units, width), lambda i, pick: (pick[0], 0, 0))
    return call(
        functools.partial(pack_kernel, tasks),
        jax.ShapeDtypeStruct((rows, width), BF),
        grid_spec=pltpu.PrefetchScalarGridSpec(
            num_scalar_prefetch=1,
            grid=(1,),
            in_specs=[block, block, pl.BlockSpec(route_gate.shape, lambda i, p: (0, 0))],
            out_specs=pl.BlockSpec((rows, width), lambda i, p: (0, 0)),
        ),
        name="pack",
    )(pick, shared_in, shared_out, route_gate)


def dispatch_kernel(chips, depth, me_ref, cap_ref, r0_ref, r1_ref, t0_ref, t1_ref, *outs):
    rows_ref = outs[chips]
    me = me_ref[0]
    count = r0_ref.shape[1]
    experts = 2 * chips
    ids = lax.broadcasted_iota(I32, (experts, count), 0)
    limit = jnp.zeros((experts, count), F32)
    for q in range(experts):
        limit = jnp.where(ids == q, cap_ref[q ^ me].astype(F32), limit)
    earlier = lax.broadcasted_iota(I32, (count, count), 0) < lax.broadcasted_iota(
        I32, (count, count), 1
    )
    upper = jnp.where(earlier, 1.0, 0.0).astype(BF)
    slot = lax.broadcasted_iota(I32, (depth, count), 0).astype(F32)
    codes, keeps = [], []
    for side, (routes, tokens) in enumerate(((r0_ref, t0_ref), (r1_ref, t1_ref))):
        rel = routes[...] ^ me
        named = [rel[k : k + 1] == ids for k in range(rel.shape[0])]
        chosen = functools.reduce(jnp.logical_or, named)
        before = jnp.dot(jnp.where(chosen, 1.0, 0.0).astype(BF), upper, preferred_element_type=F32)
        kept = jnp.logical_and(chosen, before < limit)
        ranked = jnp.where(kept, before, -1.0)
        table = jnp.concatenate(
            [
                jnp.where(ranked[2 * m : 2 * m + 1] == slot, 1.0, 0.0).astype(BF)
                for m in range(chips)
            ],
            axis=0,
        )
        picked = jnp.dot(table, tokens[...], preferred_element_type=F32).astype(BF)
        for m in range(chips):
            outs[m][side * depth : (side + 1) * depth] = picked[m * depth : (m + 1) * depth]
        for k, here in enumerate(named):
            rank = jnp.sum(jnp.where(here, ranked, 0.0), axis=0, keepdims=True)
            keep = rank >= 0.0
            mine = jnp.logical_and(keep, (rel[k : k + 1] & 1) == 0)
            place = ((rel[k : k + 1] >> 1) * depth).astype(F32) + rank
            codes.append(jnp.where(mine, place, -1.0))
            if side == 0:
                keeps.append(jnp.where(keep, 1.0, 0.0))
    blank = jnp.zeros((rows_ref.shape[0] - len(codes) - len(keeps), count), F32)
    rows_ref[...] = jnp.concatenate(codes + keeps + [blank], axis=0)


def dispatch(me, capacity, r0, r1, t0, t1, depth):
    chips = capacity.shape[0] // 2
    count, width = t0.shape
    smem = pl.BlockSpec(memory_space=pltpu.SMEM)
    vmem = pl.BlockSpec(memory_space=pltpu.VMEM)
    return call(
        functools.partial(dispatch_kernel, chips, depth),
        [jax.ShapeDtypeStruct((2 * depth, width), BF)] * chips
        + [jax.ShapeDtypeStruct((8, count), F32)],
        in_specs=[smem, smem] + [vmem] * 4,
        out_specs=[vmem] * (chips + 1),
        cost_estimate=cost(4 * chips * depth * count * width, 6 * count * width),
        name="dispatch",
    )(me, capacity, r0, r1, t0, t1)


def expert_kernel(blocks, w1_ref, w2_ref, *refs):
    ins, outs, x_ref, acc_ref = refs[:blocks], refs[blocks : 2 * blocks], refs[-2], refs[-1]
    step = pl.program_id(0)
    rows = ins[0].shape[0]

    @pl.when(step == 0)
    def _():
        for i in range(blocks):
            x_ref[i * rows : (i + 1) * rows] = ins[i][...]

    hidden = jax.nn.gelu(jnp.dot(x_ref[...], w1_ref[...], preferred_element_type=F32)).astype(BF)
    part = jnp.dot(hidden, w2_ref[...], preferred_element_type=F32)

    @pl.when(step == 0)
    def _():
        acc_ref[...] = part

    @pl.when(step > 0)
    def _():
        acc_ref[...] += part

    @pl.when(step == pl.num_programs(0) - 1)
    def _():
        for i in range(blocks):
            outs[i][...] = acc_ref[i * rows : (i + 1) * rows].astype(BF)


def expert(w1, w2, xs, tile=512):
    width, units = w1.shape
    tile = min(tile, units)
    rows = xs[0].shape[0]
    total = rows * len(xs)
    row_spec = whole((rows, width))
    return call(
        functools.partial(expert_kernel, len(xs)),
        [jax.ShapeDtypeStruct((rows, width), BF)] * len(xs),
        grid=(units // tile,),
        in_specs=[
            pl.BlockSpec((width, tile), lambda i: (0, i)),
            pl.BlockSpec((tile, width), lambda i: (i, 0)),
        ]
        + [row_spec] * len(xs),
        out_specs=[row_spec] * len(xs),
        scratch_shapes=[pltpu.VMEM((total, width), BF), pltpu.VMEM((total, width), F32)],
        cost_estimate=cost(4 * total * width * units, 4 * width * (units + total)),
        name="expert",
    )(w1, w2, *xs)


def shared_kernel(units, a_ref, b_ref, t0, t1, t2, t3, keep_ref, send_ref, g_ref, x_ref, acc_ref):
    step = pl.program_id(0)
    rows = t0.shape[0]

    @pl.when(step == 0)
    def _():
        for i, t in enumerate((t0, t1, t2, t3)):
            x_ref[i * rows : (i + 1) * rows] = t[...]
        acc_ref[...] = jnp.zeros_like(acc_ref)

    g_ref[0] = a_ref[0, 2 * units :]
    g_ref[1] = b_ref[0, 2 * units :]
    up = jnp.concatenate([a_ref[0, 0:units], b_ref[0, 0:units]], axis=0)
    down = jnp.concatenate([a_ref[0, units : 2 * units], b_ref[0, units : 2 * units]], axis=0)
    hidden = jax.nn.gelu(dot_t(x_ref[...], up)).astype(BF)
    acc_ref[...] += jnp.dot(hidden, down, preferred_element_type=F32)

    @pl.when(step == pl.num_programs(0) - 1)
    def _():
        keep_ref[...] = acc_ref[0 : 2 * rows].astype(BF)
        send_ref[...] = acc_ref[2 * rows :].astype(BF)


def shared(a, b, units, tokens):
    half, packed, width = a.shape
    rows = tokens[0].shape[0]
    block = pl.BlockSpec((1, packed, width), lambda i: (i, 0, 0))
    gates = packed - 2 * units
    return call(
        functools.partial(shared_kernel, units),
        [
            jax.ShapeDtypeStruct((2 * rows, width), BF),
            jax.ShapeDtypeStruct((2 * rows, width), BF),
            jax.ShapeDtypeStruct((2, half * gates, width), BF),
        ],
        grid=(half,),
        in_specs=[block, block] + [whole((rows, width))] * 4,
        out_specs=[
            whole((2 * rows, width)),
            whole((2 * rows, width)),
            pl.BlockSpec((2, gates, width), lambda i: (0, i, 0)),
        ],
        scratch_shapes=[pltpu.VMEM((4 * rows, width), BF), pltpu.VMEM((4 * rows, width), F32)],
        cost_estimate=cost(32 * rows * width * units * half, 4 * half * packed * width),
        name="shared",
    )(a, b, *tokens)


def weight_kernel(tasks, order, me_ref, pick_ref, rows_ref, r_ref, t_ref, g0_ref, g1_ref, s_ref, w_ref):
    width = t_ref.shape[1]
    count = t_ref.shape[0]
    me, pick = me_ref[0], pick_ref[0]
    rel = r_ref[...] ^ me
    tokens = t_ref[...]
    gates = g0_ref.shape[1] // (len(order) // 2)

    def logits(g):
        return dot_t(g, tokens).astype(BF).astype(F32)

    chosen = [jnp.zeros((gates, count), F32) for _ in range(2)]
    for parity, ref in ((0, g0_ref), (1, g1_ref)):
        for side in range(2):
            found = logits(ref[side])
            for p in range(len(order) // 2):
                mask = order[side * (len(order) // 2) + p] ^ parity
                for k in range(2):
                    chosen[k] = jnp.where(
                        rel[k : k + 1] == mask, found[p * gates : (p + 1) * gates], chosen[k]
                    )
    keep0 = 2 * 2
    values = [rows_ref[keep0 + k : keep0 + k + 1] * jax.nn.sigmoid(chosen[k]) for k in range(2)]
    own = []
    for j in range(2):
        gate = jnp.concatenate(
            [s_ref[j : j + 1, s * width : (s + 1) * width] for s in range(tasks)]
            + [jnp.zeros((gates - tasks, width), BF)],
            axis=0,
        )
        own.append(jax.nn.sigmoid(logits(gate)))
    total = values[0] + values[1] + own[0] + own[1]
    first = jnp.where(pick == 0, own[0], own[1])
    second = jnp.where(pick == 0, own[1], own[0])
    columns = [v / total for v in (values[0], values[1], first, second)] + [rows_ref[...]]
    high = sum(c.shape[0] for c in columns)
    full = -(-high // 128) * 128
    columns.append(jnp.zeros((full - high, count), F32))
    w_ref[...] = jnp.concatenate(columns, axis=0).T


def weights(me, pick, rows, routes, tokens, g0, g1, shared_gate, tasks, order):
    smem = pl.BlockSpec(memory_space=pltpu.SMEM)
    vmem = pl.BlockSpec(memory_space=pltpu.VMEM)
    gates = -(-tasks // PAD) * PAD
    full = -(-(4 * gates + rows.shape[0]) // 128) * 128
    return call(
        functools.partial(weight_kernel, tasks, order),
        jax.ShapeDtypeStruct((tokens.shape[0], full), F32),
        in_specs=[smem, smem] + [vmem] * 6,
        out_specs=vmem,
        cost_estimate=cost(2 * tokens.size * g0.shape[1] * 4, 4 * g0.size + 2 * tokens.size),
        name="weights",
    )(me, pick, rows, routes, tokens, g0, g1, shared_gate)


def collect_kernel(chips, first, w_ref, *refs):
    ins, mine_ref, other_ref = refs[:chips], refs[-2], refs[-1]
    depth = ins[0].shape[0] // 2
    count = w_ref.shape[0]
    ids = lax.broadcasted_iota(I32, (count, chips * depth), 1).astype(F32)
    for side, out in ((0, mine_ref), (1, other_ref)):
        rows = jnp.concatenate([r[side * depth : (side + 1) * depth] for r in ins], axis=0)
        for k in range(2):
            column = first + 2 * side + k
            table = jnp.where(w_ref[:, column : column + 1] == ids, 1.0, 0.0).astype(BF)
            out[k * count : (k + 1) * count] = jnp.dot(
                table, rows, preferred_element_type=F32
            ).astype(BF)


def collect(w, blocks, first):
    vmem = pl.BlockSpec(memory_space=pltpu.VMEM)
    count, width = w.shape[0], blocks[0].shape[1]
    slots = sum(b.shape[0] for b in blocks)
    return call(
        functools.partial(collect_kernel, len(blocks), first),
        [jax.ShapeDtypeStruct((2 * count, width), BF)] * 2,
        in_specs=[vmem] * (1 + len(blocks)),
        out_specs=[vmem] * 2,
        cost_estimate=cost(4 * count * slots * width, 2 * slots * width + 8 * count * width),
        name="collect",
    )(w, *blocks)


def mix_kernel(tasks, gates, w_ref, a0, a1, b0, b1, s0, s1, x_ref, out_ref):
    rows = [
        (a0[...] + b0[...]).astype(F32),
        (a1[...] + b1[...]).astype(F32),
        s0[...].astype(F32) + s1[...].astype(F32),
        x_ref[...].astype(F32),
    ]
    for s in range(tasks):
        mixed = None
        for j, row in enumerate(rows):
            column = j * gates + s
            term = w_ref[:, column : column + 1] * row
            mixed = term if mixed is None else mixed + term
        out_ref[s] = mixed.astype(BF)


def mix(w, mine, theirs, keep, back, far, tasks, block=64):
    count, full = w.shape
    width = far.shape[1]
    gates = -(-tasks // PAD) * PAD
    steps = count // block
    low = pl.BlockSpec((block, width), lambda i: (i, 0))
    high = pl.BlockSpec((block, width), lambda i: (i + steps, 0))
    return call(
        functools.partial(mix_kernel, tasks, gates),
        jax.ShapeDtypeStruct((tasks, count, width), BF),
        grid=(steps,),
        in_specs=[pl.BlockSpec((block, full), lambda i: (i, 0)), low, high, low, high, low, low, low],
        out_specs=pl.BlockSpec((tasks, block, width), lambda i: (0, i, 0)),
        cost_estimate=cost(8 * tasks * count * width, 2 * (tasks + 8) * count * width),
        name="mix",
    )(w, mine, mine, theirs, theirs, keep, back, far)


def on_device(
    tokens, routes, capacity, expert_in, expert_out, shared_in, shared_out, route_gate, shared_gate
):
    experts = lax.axis_size("ep")
    chips = experts // 2
    count, width = tokens.shape
    tasks = shared_gate.shape[1] // width
    units = shared_in.shape[1]
    depth = max(4, 4 * count // experts)
    me = lax.axis_index("ep").astype(I32).reshape(1)
    pick = lax.axis_index("dp").astype(I32).reshape(1)

    def swap(x, mask):
        return lax.ppermute(x, "ep", [(i, i ^ mask) for i in range(experts)])

    def across(x):
        groups = lax.axis_size("dp")
        return lax.ppermute(x, "dp", [(i, groups - 1 - i) for i in range(groups)])

    turned = routes.T
    partner_routes = swap(turned, 1)
    partner = swap(tokens, 1)
    packed = pack(pick, shared_in, shared_out, route_gate, tasks)

    *outgoing, rows = dispatch(me, capacity, turned, partner_routes, tokens, partner, depth)
    near, far = range(0, chips // 2), range(chips // 2, chips)
    arrived = {0: outgoing[0]}
    for m in list(far) + [m for m in reversed(near) if m]:
        arrived[m] = swap(outgoing[m], 2 * m)

    gathered, order, mask = packed[None], [0], experts // 2
    while mask > 2:
        gathered = jnp.concatenate([gathered, swap(gathered, mask)], axis=0)
        order = order + [o ^ mask for o in order]
        mask //= 2
    other_half = swap(gathered, mask)
    order = order + [o ^ mask for o in order]

    visitor = across(tokens)
    partner_visitor = swap(visitor, 1)

    w1, w2 = expert_in[0], expert_out[0]
    results = dict(zip(near, expert(w1, w2, [arrived[m] for m in near])))
    results.update(zip(far, expert(w1, w2, [arrived[m] for m in far])))
    back = {0: results[0]}
    for m in list(far) + [m for m in reversed(near) if m]:
        back[m] = swap(results[m], 2 * m)

    keep, send, gates = shared(
        gathered, other_half, units, (tokens, visitor, partner, partner_visitor)
    )
    other_gates = swap(gates, 1)
    summed = swap(send, 1)
    crossing = (keep[count:].astype(F32) + summed[count:].astype(F32)).astype(BF)
    far_rows = across(crossing)
    w = weights(
        me, pick, rows, turned, tokens, gates, other_gates, shared_gate, tasks, tuple(order)
    )
    mine, other = collect(w, [back[m] for m in range(chips)], 4 * (-(-tasks // PAD) * PAD))
    theirs = swap(other, 1)
    mixed = mix(w, mine, theirs, keep, summed, far_rows, tasks)
    return mixed.transpose(1, 0, 2)


def solution(mesh):
    return jax.shard_map(
        on_device,
        mesh=mesh,
        in_specs=(
            P(("dp", "ep"), None),
            P(("dp", "ep"), None),
            P(),
            P("ep", None, None),
            P("ep", None, None),
            P(None, "ep", None),
            P(None, "ep", None),
            P("ep", None),
            P(),
        ),
        out_specs=P(("dp", "ep"), None, None),
        check_vma=False,
    )
```

```python
import functools

import jax
import jax.numpy as jnp
from jax import lax
from jax.experimental import pallas as pl
from jax.experimental.pallas import tpu as pltpu
from jax.sharding import PartitionSpec as P


BF, F32, I32 = jnp.bfloat16, jnp.float32, jnp.int32
GRANT = 24 << 20
PAD = 16


def whole(shape):
    return pl.BlockSpec(shape, lambda *_: (0,) * len(shape))


def call(kernel, out_shape, **kw):
    return pl.pallas_call(
        kernel,
        out_shape=out_shape,
        compiler_params=pltpu.CompilerParams(vmem_limit_bytes=GRANT),
        **kw,
    )


def in_hbm(x):
    return pltpu.with_memory_space_constraint(x, pltpu.HBM)


def cost(flops, size):
    return pl.CostEstimate(flops=int(flops), bytes_accessed=int(size), transcendentals=0)


def dot_t(a, b):
    return lax.dot_general(a, b, (((1,), (1,)), ((), ())), preferred_element_type=F32)


def pack_kernel(tasks, me_ref, pick_ref, *refs):
    (in_ref, out_ref, gate_ref, t_ref, r_ref, c_ref, packed_ref, sent_ref, limit_ref) = refs[:9]
    gates, routes, caps, sems = refs[9:]
    units, width = in_ref.shape[1:]
    count = t_ref.shape[0]
    pick, me = pick_ref[0], me_ref[0]
    copies = [
        pltpu.make_async_copy(source, target, sems.at[i])
        for i, (source, target) in enumerate(
            (
                (r_ref, routes),
                (c_ref, caps),
                (gate_ref, gates),
                (t_ref, sent_ref.at[0:count]),
                (in_ref.at[pick], packed_ref.at[0:units]),
                (out_ref.at[pick], packed_ref.at[units : 2 * units]),
            )
        )
    ]
    for copy in copies:
        copy.start()
    for copy in copies[:3]:
        copy.wait()
    blank = jnp.zeros((PAD - routes.shape[0], count), F32)
    named = jnp.concatenate([routes[...].astype(F32), blank], axis=0).astype(BF)
    sent_ref[count:] = jnp.concatenate([named, jnp.zeros((PAD, width - count), BF)], axis=1)
    rows = [gates[:, s * width : (s + 1) * width] for s in range(tasks)]
    rows.append(jnp.zeros((packed_ref.shape[0] - 2 * units - tasks, width), BF))
    packed_ref[2 * units :] = jnp.concatenate(rows, axis=0)
    ids = lax.broadcasted_iota(I32, limit_ref.shape, 0)
    limit = jnp.zeros(limit_ref.shape, F32)
    for q in range(limit_ref.shape[0]):
        limit = jnp.where(ids == q, caps[q ^ me].astype(F32), limit)
    limit_ref[...] = limit
    for copy in copies[3:]:
        copy.wait()


def pack(me, pick, shared_in, shared_out, route_gate, tokens, routes, capacity, tasks):
    _, units, width = shared_in.shape
    count = tokens.shape[0]
    rows = 2 * units + -(-tasks // PAD) * PAD
    smem = pl.BlockSpec(memory_space=pltpu.SMEM)
    vmem = pl.BlockSpec(memory_space=pltpu.VMEM)
    return call(
        functools.partial(pack_kernel, tasks),
        [
            jax.ShapeDtypeStruct((rows, width), BF),
            jax.ShapeDtypeStruct((count + PAD, width), BF),
            jax.ShapeDtypeStruct((capacity.shape[0], count), F32),
        ],
        in_specs=[smem, smem] + [pl.BlockSpec(memory_space=pltpu.HBM)] * 6,
        out_specs=[vmem] * 3,
        scratch_shapes=[
            pltpu.VMEM(route_gate.shape, BF),
            pltpu.VMEM(routes.shape, I32),
            pltpu.SMEM(capacity.shape, I32),
            pltpu.SemaphoreType.DMA((6,)),
        ],
    )(me, pick, *map(in_hbm, (shared_in, shared_out, route_gate, tokens, routes, capacity)))


def dispatch_kernel(targets, depth, me_ref, limit_ref, t0_ref, t1_ref, *outs):
    me = me_ref[0]
    experts, count = limit_ref.shape
    ids = lax.broadcasted_iota(I32, (experts, count), 0)
    earlier = lax.broadcasted_iota(I32, (count, count), 0) < lax.broadcasted_iota(
        I32, (count, count), 1
    )
    upper = jnp.where(earlier, 1.0, 0.0).astype(BF)
    slot = lax.broadcasted_iota(I32, (depth, count), 0).astype(F32)
    codes, keeps = [], []
    for side, sent in enumerate((t0_ref, t1_ref)):
        rel = routes_of(sent, count) ^ me
        named = [rel[k : k + 1] == ids for k in range(2)]
        chosen = jnp.logical_or(*named)
        before = jnp.dot(jnp.where(chosen, 1.0, 0.0).astype(BF), upper, preferred_element_type=F32)
        kept = jnp.logical_and(chosen, before < limit_ref[...])
        ranked = jnp.where(kept, before, -1.0)
        table = jnp.concatenate(
            [
                jnp.where(ranked[2 * m : 2 * m + 1] == slot, 1.0, 0.0).astype(BF)
                for m in range(targets)
            ],
            axis=0,
        )
        picked = jnp.dot(table, sent[0:count], preferred_element_type=F32).astype(BF)
        for m in range(targets):
            outs[m][side * depth : (side + 1) * depth] = picked[m * depth : (m + 1) * depth]
        for k, here in enumerate(named):
            rank = jnp.sum(jnp.where(here, ranked, 0.0), axis=0, keepdims=True)
            keep = rank >= 0.0
            mine = jnp.logical_and(keep, (rel[k : k + 1] & 1) == 0)
            place = ((rel[k : k + 1] >> 1) * depth).astype(F32) + rank
            codes.append(jnp.where(mine, place, -1.0))
            if side == 0:
                keeps.append(jnp.where(keep, 1.0, 0.0))
    if len(outs) > targets:
        blank = jnp.zeros((8 - len(codes) - len(keeps), count), F32)
        outs[targets][...] = jnp.concatenate(codes + keeps + [blank], axis=0)


def routes_of(sent, count):
    return sent[count:, 0:count].astype(F32)[0:2].astype(I32)


def dispatch(me, limit, t0, t1, depth, slots):
    targets = limit.shape[0] // 4
    count, width = limit.shape[1], t0.shape[1]
    smem = pl.BlockSpec(memory_space=pltpu.SMEM)
    vmem = pl.BlockSpec(memory_space=pltpu.VMEM)
    return call(
        functools.partial(dispatch_kernel, targets, depth),
        [jax.ShapeDtypeStruct((2 * depth, width), BF)] * targets
        + [jax.ShapeDtypeStruct((8, count), F32)] * slots,
        in_specs=[smem] + [vmem] * 3,
        out_specs=[vmem] * (targets + slots),
        cost_estimate=cost(4 * targets * depth * count * width, 6 * count * width),
    )(me, limit, t0, t1)


def load_kernel(a_ref, b_ref, a_out, b_out, sems):
    parts = sems.shape[1]
    copies = []
    for j, (source, target) in enumerate(((a_ref, a_out), (b_ref, b_out))):
        rows = source.shape[0] // parts
        for i in range(parts):
            piece = pl.ds(i * rows, rows)
            copies.append(
                pltpu.make_async_copy(source.at[piece], target.at[piece], sems.at[j, i])
            )
    for copy in copies:
        copy.start()
    for copy in copies:
        copy.wait()


def load(a, b):
    return call(
        load_kernel,
        [jax.ShapeDtypeStruct(a.shape, a.dtype), jax.ShapeDtypeStruct(b.shape, b.dtype)],
        in_specs=[pl.BlockSpec(memory_space=pltpu.HBM)] * 2,
        out_specs=[pl.BlockSpec(memory_space=pltpu.VMEM)] * 2,
        scratch_shapes=[pltpu.SemaphoreType.DMA((2, 4))],
        cost_estimate=cost(0, 4 * (a.size + b.size)),
    )(in_hbm(a), in_hbm(b))


def expert_kernel(blocks, w1_ref, w2_ref, *refs):
    ins, outs, x_ref, acc_ref = refs[:blocks], refs[blocks : 2 * blocks], refs[-2], refs[-1]
    step = pl.program_id(0)
    rows = ins[0].shape[0]

    @pl.when(step == 0)
    def _():
        for i in range(blocks):
            x_ref[i * rows : (i + 1) * rows] = ins[i][...]

    hidden = jax.nn.gelu(jnp.dot(x_ref[...], w1_ref[...], preferred_element_type=F32)).astype(BF)
    part = jnp.dot(hidden, w2_ref[...], preferred_element_type=F32)

    @pl.when(step == 0)
    def _():
        acc_ref[...] = part

    @pl.when(step > 0)
    def _():
        acc_ref[...] += part

    @pl.when(step == pl.num_programs(0) - 1)
    def _():
        for i in range(blocks):
            outs[i][...] = acc_ref[i * rows : (i + 1) * rows].astype(BF)


def expert(w1, w2, xs, tile=1024):
    width, units = w1.shape
    tile = min(tile, units)
    rows = xs[0].shape[0]
    total = rows * len(xs)
    row_spec = whole((rows, width))
    return call(
        functools.partial(expert_kernel, len(xs)),
        [jax.ShapeDtypeStruct((rows, width), BF)] * len(xs),
        grid=(units // tile,),
        in_specs=[
            pl.BlockSpec((width, tile), lambda i: (0, i)),
            pl.BlockSpec((tile, width), lambda i: (i, 0)),
        ]
        + [row_spec] * len(xs),
        out_specs=[row_spec] * len(xs),
        scratch_shapes=[pltpu.VMEM((total, width), BF), pltpu.VMEM((total, width), F32)],
        cost_estimate=cost(4 * total * width * units, 4 * width * (units + total)),
    )(w1, w2, *xs)


def shared_kernel(shards, units, last, group, *refs):
    ins, tokens, refs = refs[:shards], refs[shards : shards + 4], refs[shards + 4 :]
    rows = refs[-1].shape[0] // 4
    count = rows
    x_ref = refs[-1]
    for i, t in enumerate(tokens):
        x_ref[i * rows : (i + 1) * rows] = t[0:count]
    total = None
    for first in range(0, shards, group):
        part = ins[first : first + group]
        up = jnp.concatenate([w[0:units] for w in part], axis=0)
        down = jnp.concatenate([w[units : 2 * units] for w in part], axis=0)
        hidden = jax.nn.gelu(dot_t(x_ref[...], up)).astype(BF)
        term = jnp.dot(hidden, down, preferred_element_type=F32)
        total = term if total is None else total + term
    gates = jnp.concatenate([w[2 * units :] for w in ins], axis=0)
    if last:
        before, early, keep_ref, send_ref = refs[:4]
        total = total + before[...]
        keep_ref[...] = total[0 : 2 * rows].astype(BF)
        send_ref[0 : 2 * rows] = total[2 * rows :].astype(BF)
        send_ref[2 * rows : 2 * rows + gates.shape[0]] = early[...]
        send_ref[2 * rows + gates.shape[0] :] = gates
    else:
        refs[0][...] = total
        refs[1][...] = gates


def shared(shards, units, tokens, count, carried=()):
    width = shards[0].shape[1]
    gates = len(shards) * (shards[0].shape[0] - 2 * units)
    vmem = pl.BlockSpec(memory_space=pltpu.VMEM)
    if carried:
        shapes = [((2 * count, width), BF), ((2 * count + 2 * gates, width), BF)]
    else:
        shapes = [((4 * count, width), F32), ((gates, width), BF)]
    group = max(1, min(len(shards), 256 // units))
    return call(
        functools.partial(shared_kernel, len(shards), units, bool(carried), group),
        [jax.ShapeDtypeStruct(*shape) for shape in shapes],
        in_specs=[vmem] * (len(shards) + 4 + len(carried)),
        out_specs=[vmem] * 2,
        scratch_shapes=[pltpu.VMEM((4 * count, width), BF)],
        cost_estimate=cost(
            16 * count * width * units * len(shards), 4 * len(shards) * units * width
        ),
    )(*shards, *tokens, *carried)


def weight_kernel(tasks, order, me_ref, pick_ref, rows_ref, t_ref, g0_ref, g1_ref, s_ref, w_ref):
    count = rows_ref.shape[1]
    width = t_ref.shape[1]
    me, pick = me_ref[0], pick_ref[0]
    rel = routes_of(t_ref, count) ^ me
    tokens = t_ref[0:count]
    gates = -(-tasks // PAD) * PAD
    total = len(order) * gates

    def logits(g):
        return dot_t(g, tokens).astype(BF).astype(F32)

    chosen = [jnp.zeros((gates, count), F32) for _ in range(2)]
    for parity, ref in ((0, g0_ref), (1, g1_ref)):
        found = logits(ref[ref.shape[0] - total :])
        for p, q in enumerate(order):
            for k in range(2):
                chosen[k] = jnp.where(
                    rel[k : k + 1] == q ^ parity, found[p * gates : (p + 1) * gates], chosen[k]
                )
    values = [rows_ref[4 + k : 5 + k] * jax.nn.sigmoid(chosen[k]) for k in range(2)]
    own = []
    for j in range(2):
        gate = jnp.concatenate(
            [s_ref[j : j + 1, s * width : (s + 1) * width] for s in range(tasks)]
            + [jnp.zeros((gates - tasks, width), BF)],
            axis=0,
        )
        own.append(jax.nn.sigmoid(logits(gate)))
    total = values[0] + values[1] + own[0] + own[1]
    first = jnp.where(pick == 0, own[0], own[1])
    second = jnp.where(pick == 0, own[1], own[0])
    columns = [v / total for v in (values[0], values[1], first, second)] + [rows_ref[...]]
    high = sum(c.shape[0] for c in columns)
    full = -(-high // 128) * 128
    columns.append(jnp.zeros((full - high, count), F32))
    w_ref[...] = jnp.concatenate(columns, axis=0).T


def weights(me, pick, rows, sent, g0, g1, shared_gate, tasks, order):
    smem = pl.BlockSpec(memory_space=pltpu.SMEM)
    vmem = pl.BlockSpec(memory_space=pltpu.VMEM)
    gates = -(-tasks // PAD) * PAD
    full = -(-(4 * gates + rows.shape[0]) // 128) * 128
    return call(
        functools.partial(weight_kernel, tasks, order),
        jax.ShapeDtypeStruct((rows.shape[1], full), F32),
        in_specs=[smem, smem] + [vmem] * 5,
        out_specs=vmem,
        cost_estimate=cost(8 * sent.size * gates * len(order), 4 * g0.size + 2 * sent.size),
    )(me, pick, rows, sent, g0, g1, shared_gate)


def collect_kernel(chips, first, w_ref, *refs):
    ins, mine_ref, other_ref = refs[:chips], refs[-2], refs[-1]
    depth = ins[0].shape[0] // 2
    count = w_ref.shape[0]
    ids = lax.broadcasted_iota(I32, (count, chips * depth), 1).astype(F32)
    for side, out in ((0, mine_ref), (1, other_ref)):
        rows = jnp.concatenate([r[side * depth : (side + 1) * depth] for r in ins], axis=0)
        for k in range(2):
            column = first + 2 * side + k
            table = jnp.where(w_ref[:, column : column + 1] == ids, 1.0, 0.0).astype(BF)
            out[k * count : (k + 1) * count] = jnp.dot(
                table, rows, preferred_element_type=F32
            ).astype(BF)


def collect(w, blocks, first):
    vmem = pl.BlockSpec(memory_space=pltpu.VMEM)
    count, width = w.shape[0], blocks[0].shape[1]
    slots = sum(b.shape[0] for b in blocks)
    return call(
        functools.partial(collect_kernel, len(blocks), first),
        [jax.ShapeDtypeStruct((2 * count, width), BF)] * 2,
        in_specs=[vmem] * (1 + len(blocks)),
        out_specs=[vmem] * 2,
        cost_estimate=cost(4 * count * slots * width, 2 * slots * width + 8 * count * width),
    )(w, *blocks)


def mix_kernel(tasks, gates, w_ref, a0, a1, b0, b1, s0, s1, x_ref, out_ref):
    rows = [
        (a0[...] + b0[...]).astype(F32),
        (a1[...] + b1[...]).astype(F32),
        s0[...].astype(F32) + s1[...].astype(F32),
        x_ref[...].astype(F32),
    ]
    for s in range(tasks):
        mixed = None
        for j, row in enumerate(rows):
            column = j * gates + s
            term = w_ref[:, column : column + 1] * row
            mixed = term if mixed is None else mixed + term
        out_ref[s] = mixed.astype(BF)


def mix(w, mine, theirs, keep, back, far, tasks, block=64):
    count, full = w.shape
    width = far.shape[1]
    gates = -(-tasks // PAD) * PAD
    steps = count // block
    low = pl.BlockSpec((block, width), lambda i: (i, 0))
    high = pl.BlockSpec((block, width), lambda i: (i + steps, 0))
    return call(
        functools.partial(mix_kernel, tasks, gates),
        jax.ShapeDtypeStruct((tasks, count, width), BF),
        grid=(steps,),
        in_specs=[pl.BlockSpec((block, full), lambda i: (i, 0)), low, high, low, high, low, low, low],
        out_specs=pl.BlockSpec((tasks, block, width), lambda i: (0, i, 0)),
        cost_estimate=cost(8 * tasks * count * width, 2 * (tasks + 8) * count * width),
    )(w, mine, mine, theirs, theirs, keep, back, far)


def on_device(
    tokens, routes, capacity, expert_in, expert_out, shared_in, shared_out, route_gate, shared_gate
):
    experts = lax.axis_size("ep")
    chips = experts // 2
    count, width = tokens.shape
    tasks = shared_gate.shape[1] // width
    units = shared_in.shape[1]
    depth = max(4, 4 * count // experts)
    me = lax.axis_index("ep").astype(I32).reshape(1)
    pick = lax.axis_index("dp").astype(I32).reshape(1)

    def swap(x, mask):
        return lax.ppermute(x, "ep", [(i, i ^ mask) for i in range(experts)])

    def across(x):
        groups = lax.axis_size("dp")
        return lax.ppermute(x, "dp", [(i, groups - 1 - i) for i in range(groups)])

    half = chips // 2
    near = near_masks(chips)
    turned = routes.T
    packed, sent, limit = pack(
        me, pick, shared_in, shared_out, route_gate, tokens, turned, capacity, tasks
    )
    opposite = swap(sent, half * 2)
    partner = swap(sent, 1)
    opposite_partner = swap(opposite, 1)
    visitor = across(tokens)
    partner_visitor = swap(visitor, 1)

    shards = {0: packed}
    for q in range(1, chips):
        shards[q] = swap(shards[q & (q - 1)], 2 * (q & -q))

    *outgoing, rows = dispatch(me, limit, sent, partner, depth, 1)
    passing = dispatch(me, limit, opposite, opposite_partner, depth, 0)
    arrived = {0: outgoing[0], half: passing[0]}
    for m in near:
        arrived[m] = swap(outgoing[m], 2 * m)
        arrived[half + m] = swap(passing[m], 2 * m)

    w1, w2 = load(expert_in[0], expert_out[0])
    early, late = [0, half] + near, [half + m for m in near]
    results = dict(zip(early, expert(w1, w2, [arrived[m] for m in early])))
    results.update(zip(late, expert(w1, w2, [arrived[m] for m in late])))
    back = {0: results[0]}
    for m in early[1:] + late:
        back[m] = swap(results[m], 2 * m)

    samples = (sent, visitor, partner, partner_visitor)
    low, high = range(half), range(half, chips)
    part = shared([shards[q] for q in low], units, samples, count)
    keep, send = shared([shards[q] for q in high], units, samples, count, part)
    summed = swap(send, 1)
    crossing = (keep[count:].astype(F32) + summed[count : 2 * count].astype(F32)).astype(BF)
    far_rows = across(crossing)
    order = tuple(2 * q for q in range(chips))
    w = weights(me, pick, rows, sent, send, summed, shared_gate, tasks, order)
    mine, other = collect(w, [back[m] for m in range(chips)], 4 * (-(-tasks // PAD) * PAD))
    theirs = swap(other, 1)
    mixed = mix(w, mine, theirs, keep, summed, far_rows, tasks)
    return mixed.transpose(1, 0, 2)


def near_masks(chips):
    return list(range(chips // 2 - 1, 0, -1))


def solution(mesh):
    return jax.shard_map(
        on_device,
        mesh=mesh,
        in_specs=(
            P(("dp", "ep"), None),
            P(("dp", "ep"), None),
            P(),
            P("ep", None, None),
            P("ep", None, None),
            P(None, "ep", None),
            P(None, "ep", None),
            P("ep", None),
            P(),
        ),
        out_specs=P(("dp", "ep"), None, None),
        check_vma=False,
    )
```

```python
import functools

import jax
import jax.numpy as jnp
from jax import lax
from jax.experimental import pallas as pl
from jax.experimental.pallas import tpu as pltpu
from jax.sharding import PartitionSpec as P


BF, F32, I32 = jnp.bfloat16, jnp.float32, jnp.int32
GRANT = 24 << 20
PAD = 16


def whole(shape):
    return pl.BlockSpec(shape, lambda *_: (0,) * len(shape))


def call(kernel, out_shape, **kw):
    return pl.pallas_call(
        kernel,
        out_shape=out_shape,
        compiler_params=pltpu.CompilerParams(vmem_limit_bytes=GRANT),
        **kw,
    )


def in_hbm(x):
    return pltpu.with_memory_space_constraint(x, pltpu.HBM)


def cost(flops, size):
    return pl.CostEstimate(flops=int(flops), bytes_accessed=int(size), transcendentals=0)


def dot_t(a, b):
    return lax.dot_general(a, b, (((1,), (1,)), ((), ())), preferred_element_type=F32)


def pack_kernel(tasks, me_ref, pick_ref, *refs):
    (in_ref, out_ref, gate_ref, t_ref, r_ref, c_ref, packed_ref, sent_ref, limit_ref) = refs[:9]
    gates, routes, caps, sems = refs[9:]
    units, width = in_ref.shape[1:]
    count = t_ref.shape[0]
    pick, me = pick_ref[0], me_ref[0]
    copies = [
        pltpu.make_async_copy(source, target, sems.at[i])
        for i, (source, target) in enumerate(
            (
                (r_ref, routes),
                (c_ref, caps),
                (gate_ref, gates),
                (t_ref, sent_ref.at[0:count]),
                (in_ref.at[pick], packed_ref.at[0:units]),
                (out_ref.at[pick], packed_ref.at[units : 2 * units]),
            )
        )
    ]
    for copy in copies:
        copy.start()
    for copy in copies[:3]:
        copy.wait()
    blank = jnp.zeros((PAD - routes.shape[0], count), F32)
    named = jnp.concatenate([routes[...].astype(F32), blank], axis=0).astype(BF)
    sent_ref[count:] = jnp.concatenate([named, jnp.zeros((PAD, width - count), BF)], axis=1)
    rows = [gates[:, s * width : (s + 1) * width] for s in range(tasks)]
    rows.append(jnp.zeros((packed_ref.shape[0] - 2 * units - tasks, width), BF))
    packed_ref[2 * units :] = jnp.concatenate(rows, axis=0)
    ids = lax.broadcasted_iota(I32, limit_ref.shape, 0)
    limit = jnp.zeros(limit_ref.shape, F32)
    for q in range(limit_ref.shape[0]):
        limit = jnp.where(ids == q, caps[q ^ me].astype(F32), limit)
    limit_ref[...] = limit
    for copy in copies[3:]:
        copy.wait()


def pack(me, pick, shared_in, shared_out, route_gate, tokens, routes, capacity, tasks):
    _, units, width = shared_in.shape
    count = tokens.shape[0]
    rows = 2 * units + -(-tasks // PAD) * PAD
    smem = pl.BlockSpec(memory_space=pltpu.SMEM)
    vmem = pl.BlockSpec(memory_space=pltpu.VMEM)
    return call(
        functools.partial(pack_kernel, tasks),
        [
            jax.ShapeDtypeStruct((rows, width), BF),
            jax.ShapeDtypeStruct((count + PAD, width), BF),
            jax.ShapeDtypeStruct((capacity.shape[0], count), F32),
        ],
        in_specs=[smem, smem] + [pl.BlockSpec(memory_space=pltpu.HBM)] * 6,
        out_specs=[vmem] * 3,
        scratch_shapes=[
            pltpu.VMEM(route_gate.shape, BF),
            pltpu.VMEM(routes.shape, I32),
            pltpu.SMEM(capacity.shape, I32),
            pltpu.SemaphoreType.DMA((6,)),
        ],
    )(me, pick, *map(in_hbm, (shared_in, shared_out, route_gate, tokens, routes, capacity)))


def dispatch_kernel(targets, depth, me_ref, limit_ref, t0_ref, t1_ref, *outs):
    me = me_ref[0]
    experts, count = limit_ref.shape
    ids = lax.broadcasted_iota(I32, (experts, count), 0)
    earlier = lax.broadcasted_iota(I32, (count, count), 0) < lax.broadcasted_iota(
        I32, (count, count), 1
    )
    upper = jnp.where(earlier, 1.0, 0.0).astype(BF)
    slot = lax.broadcasted_iota(I32, (depth, count), 0).astype(F32)
    codes, keeps = [], []
    for side, sent in enumerate((t0_ref, t1_ref)):
        rel = routes_of(sent, count) ^ me
        named = [rel[k : k + 1] == ids for k in range(2)]
        chosen = jnp.logical_or(*named)
        before = jnp.dot(jnp.where(chosen, 1.0, 0.0).astype(BF), upper, preferred_element_type=F32)
        kept = jnp.logical_and(chosen, before < limit_ref[...])
        ranked = jnp.where(kept, before, -1.0)
        table = jnp.concatenate(
            [
                jnp.where(ranked[2 * m : 2 * m + 1] == slot, 1.0, 0.0).astype(BF)
                for m in range(targets)
            ],
            axis=0,
        )
        picked = jnp.dot(table, sent[0:count], preferred_element_type=F32).astype(BF)
        for m in range(targets):
            outs[m][side * depth : (side + 1) * depth] = picked[m * depth : (m + 1) * depth]
        for k, here in enumerate(named):
            rank = jnp.sum(jnp.where(here, ranked, 0.0), axis=0, keepdims=True)
            keep = rank >= 0.0
            mine = jnp.logical_and(keep, (rel[k : k + 1] & 1) == 0)
            place = ((rel[k : k + 1] >> 1) * depth).astype(F32) + rank
            codes.append(jnp.where(mine, place, -1.0))
            if side == 0:
                keeps.append(jnp.where(keep, 1.0, 0.0))
    if len(outs) > targets:
        blank = jnp.zeros((8 - len(codes) - len(keeps), count), F32)
        outs[targets][...] = jnp.concatenate(codes + keeps + [blank], axis=0)


def routes_of(sent, count):
    return sent[count:, 0:count].astype(F32)[0:2].astype(I32)


def dispatch(me, limit, t0, t1, depth, slots):
    targets = limit.shape[0] // 4
    count, width = limit.shape[1], t0.shape[1]
    smem = pl.BlockSpec(memory_space=pltpu.SMEM)
    vmem = pl.BlockSpec(memory_space=pltpu.VMEM)
    return call(
        functools.partial(dispatch_kernel, targets, depth),
        [jax.ShapeDtypeStruct((2 * depth, width), BF)] * targets
        + [jax.ShapeDtypeStruct((8, count), F32)] * slots,
        in_specs=[smem] + [vmem] * 3,
        out_specs=[vmem] * (targets + slots),
        cost_estimate=cost(4 * targets * depth * count * width, 6 * count * width),
    )(me, limit, t0, t1)


def load_kernel(a_ref, b_ref, a_out, b_out, sems):
    parts = sems.shape[1]
    copies = []
    for j, (source, target) in enumerate(((a_ref, a_out), (b_ref, b_out))):
        rows = source.shape[0] // parts
        for i in range(parts):
            piece = pl.ds(i * rows, rows)
            copies.append(
                pltpu.make_async_copy(source.at[piece], target.at[piece], sems.at[j, i])
            )
    for copy in copies:
        copy.start()
    for copy in copies:
        copy.wait()


def load(a, b):
    return call(
        load_kernel,
        [jax.ShapeDtypeStruct(a.shape, a.dtype), jax.ShapeDtypeStruct(b.shape, b.dtype)],
        in_specs=[pl.BlockSpec(memory_space=pltpu.HBM)] * 2,
        out_specs=[pl.BlockSpec(memory_space=pltpu.VMEM)] * 2,
        scratch_shapes=[pltpu.SemaphoreType.DMA((2, 4))],
        cost_estimate=cost(0, 4 * (a.size + b.size)),
    )(in_hbm(a), in_hbm(b))


def expert_kernel(blocks, w1_ref, w2_ref, *refs):
    ins, outs, x_ref, acc_ref = refs[:blocks], refs[blocks : 2 * blocks], refs[-2], refs[-1]
    step = pl.program_id(0)
    rows = ins[0].shape[0]

    @pl.when(step == 0)
    def _():
        for i in range(blocks):
            x_ref[i * rows : (i + 1) * rows] = ins[i][...]

    hidden = jax.nn.gelu(jnp.dot(x_ref[...], w1_ref[...], preferred_element_type=F32)).astype(BF)
    part = jnp.dot(hidden, w2_ref[...], preferred_element_type=F32)

    @pl.when(step == 0)
    def _():
        acc_ref[...] = part

    @pl.when(step > 0)
    def _():
        acc_ref[...] += part

    @pl.when(step == pl.num_programs(0) - 1)
    def _():
        for i in range(blocks):
            outs[i][...] = acc_ref[i * rows : (i + 1) * rows].astype(BF)


def expert(w1, w2, xs, tile=1024):
    width, units = w1.shape
    tile = min(tile, units)
    rows = xs[0].shape[0]
    total = rows * len(xs)
    row_spec = whole((rows, width))
    return call(
        functools.partial(expert_kernel, len(xs)),
        [jax.ShapeDtypeStruct((rows, width), BF)] * len(xs),
        grid=(units // tile,),
        in_specs=[
            pl.BlockSpec((width, tile), lambda i: (0, i)),
            pl.BlockSpec((tile, width), lambda i: (i, 0)),
        ]
        + [row_spec] * len(xs),
        out_specs=[row_spec] * len(xs),
        scratch_shapes=[pltpu.VMEM((total, width), BF), pltpu.VMEM((total, width), F32)],
        cost_estimate=cost(4 * total * width * units, 4 * width * (units + total)),
    )(w1, w2, *xs)


def shared_kernel(shards, units, group, start, gated, count, *refs):
    ins, refs = refs[:shards], refs[shards:]
    x_ref = refs[-1]
    blocks = x_ref.shape[0] // count
    for i in range(blocks):
        x_ref[i * count : (i + 1) * count] = refs[i][0:count]
    refs = refs[blocks:-1]
    total = None
    for first in range(0, shards, group):
        part = ins[first : first + group]
        up = jnp.concatenate([w[0:units] for w in part], axis=0)
        down = jnp.concatenate([w[units : 2 * units] for w in part], axis=0)
        hidden = jax.nn.gelu(dot_t(x_ref[...], up)).astype(BF)
        term = jnp.dot(hidden, down, preferred_element_type=F32)
        total = term if total is None else total + term
    if start is None:
        refs[0][...] = total
        refs[1][...] = jnp.concatenate([w[2 * units :] for w in ins], axis=0)
        return
    before, early, keep_ref, send_ref = refs
    total = total + before[start : start + blocks * count]
    keep_ref[...] = total[0:count].astype(BF)
    send_ref[0:count] = total[count:].astype(BF)
    if gated:
        gates = jnp.concatenate([early[...]] + [w[2 * units :] for w in ins], axis=0)
        send_ref[count:] = gates


def shared(shards, units, tokens, count, carried=(), start=None, gated=False):
    width = shards[0].shape[1]
    gates = len(shards) * (shards[0].shape[0] - 2 * units)
    vmem = pl.BlockSpec(memory_space=pltpu.VMEM)
    if carried:
        extra = 2 * gates if gated else 0
        shapes = [((count, width), BF), ((count + extra, width), BF)]
    else:
        shapes = [((len(tokens) * count, width), F32), ((gates, width), BF)]
    group = max(1, min(len(shards), 256 // units))
    return call(
        functools.partial(shared_kernel, len(shards), units, group, start, gated, count),
        [jax.ShapeDtypeStruct(*shape) for shape in shapes],
        in_specs=[vmem] * (len(shards) + len(tokens) + len(carried)),
        out_specs=[vmem] * 2,
        scratch_shapes=[pltpu.VMEM((len(tokens) * count, width), BF)],
        cost_estimate=cost(
            4 * len(tokens) * count * width * units * len(shards), 4 * len(shards) * units * width
        ),
    )(*shards, *tokens, *carried)


def weight_kernel(tasks, order, me_ref, pick_ref, rows_ref, t_ref, g0_ref, g1_ref, s_ref, w_ref):
    count = rows_ref.shape[1]
    width = t_ref.shape[1]
    me, pick = me_ref[0], pick_ref[0]
    rel = routes_of(t_ref, count) ^ me
    tokens = t_ref[0:count]
    gates = -(-tasks // PAD) * PAD
    total = len(order) * gates

    def logits(g):
        return dot_t(g, tokens).astype(BF).astype(F32)

    chosen = [jnp.zeros((gates, count), F32) for _ in range(2)]
    for parity, ref in ((0, g0_ref), (1, g1_ref)):
        found = logits(ref[ref.shape[0] - total :])
        for p, q in enumerate(order):
            for k in range(2):
                chosen[k] = jnp.where(
                    rel[k : k + 1] == q ^ parity, found[p * gates : (p + 1) * gates], chosen[k]
                )
    values = [rows_ref[4 + k : 5 + k] * jax.nn.sigmoid(chosen[k]) for k in range(2)]
    own = []
    for j in range(2):
        gate = jnp.concatenate(
            [s_ref[j : j + 1, s * width : (s + 1) * width] for s in range(tasks)]
            + [jnp.zeros((gates - tasks, width), BF)],
            axis=0,
        )
        own.append(jax.nn.sigmoid(logits(gate)))
    total = values[0] + values[1] + own[0] + own[1]
    first = jnp.where(pick == 0, own[0], own[1])
    second = jnp.where(pick == 0, own[1], own[0])
    columns = [v / total for v in (values[0], values[1], first, second)] + [rows_ref[...]]
    high = sum(c.shape[0] for c in columns)
    full = -(-high // 128) * 128
    columns.append(jnp.zeros((full - high, count), F32))
    w_ref[...] = jnp.concatenate(columns, axis=0).T


def weights(me, pick, rows, sent, g0, g1, shared_gate, tasks, order):
    smem = pl.BlockSpec(memory_space=pltpu.SMEM)
    vmem = pl.BlockSpec(memory_space=pltpu.VMEM)
    gates = -(-tasks // PAD) * PAD
    full = -(-(4 * gates + rows.shape[0]) // 128) * 128
    return call(
        functools.partial(weight_kernel, tasks, order),
        jax.ShapeDtypeStruct((rows.shape[1], full), F32),
        in_specs=[smem, smem] + [vmem] * 5,
        out_specs=vmem,
        cost_estimate=cost(8 * sent.size * gates * len(order), 4 * g0.size + 2 * sent.size),
    )(me, pick, rows, sent, g0, g1, shared_gate)


def collect_kernel(chips, first, w_ref, *refs):
    ins, mine_ref, other_ref = refs[:chips], refs[-2], refs[-1]
    depth = ins[0].shape[0] // 2
    count = w_ref.shape[0]
    ids = lax.broadcasted_iota(I32, (count, chips * depth), 1).astype(F32)
    for side, out in ((0, mine_ref), (1, other_ref)):
        rows = jnp.concatenate([r[side * depth : (side + 1) * depth] for r in ins], axis=0)
        for k in range(2):
            column = first + 2 * side + k
            table = jnp.where(w_ref[:, column : column + 1] == ids, 1.0, 0.0).astype(BF)
            out[k * count : (k + 1) * count] = jnp.dot(
                table, rows, preferred_element_type=F32
            ).astype(BF)


def collect(w, blocks, first):
    vmem = pl.BlockSpec(memory_space=pltpu.VMEM)
    count, width = w.shape[0], blocks[0].shape[1]
    slots = sum(b.shape[0] for b in blocks)
    return call(
        functools.partial(collect_kernel, len(blocks), first),
        [jax.ShapeDtypeStruct((2 * count, width), BF)] * 2,
        in_specs=[vmem] * (1 + len(blocks)),
        out_specs=[vmem] * 2,
        cost_estimate=cost(4 * count * slots * width, 2 * slots * width + 8 * count * width),
    )(w, *blocks)


def mix_kernel(tasks, gates, w_ref, a0, a1, b0, b1, s0, s1, x_ref, out_ref):
    rows = [
        (a0[...] + b0[...]).astype(F32),
        (a1[...] + b1[...]).astype(F32),
        s0[...].astype(F32) + s1[...].astype(F32),
        x_ref[...].astype(F32),
    ]
    for s in range(tasks):
        mixed = None
        for j, row in enumerate(rows):
            column = j * gates + s
            term = w_ref[:, column : column + 1] * row
            mixed = term if mixed is None else mixed + term
        out_ref[s] = mixed.astype(BF)


def mix(w, mine, theirs, keep, back, far, tasks, block=64):
    count, full = w.shape
    width = far.shape[1]
    gates = -(-tasks // PAD) * PAD
    steps = count // block
    low = pl.BlockSpec((block, width), lambda i: (i, 0))
    high = pl.BlockSpec((block, width), lambda i: (i + steps, 0))
    return call(
        functools.partial(mix_kernel, tasks, gates),
        jax.ShapeDtypeStruct((tasks, count, width), BF),
        grid=(steps,),
        in_specs=[pl.BlockSpec((block, full), lambda i: (i, 0)), low, high, low, high, low, low, low],
        out_specs=pl.BlockSpec((tasks, block, width), lambda i: (0, i, 0)),
        cost_estimate=cost(8 * tasks * count * width, 2 * (tasks + 8) * count * width),
    )(w, mine, mine, theirs, theirs, keep, back, far)


def on_device(
    tokens, routes, capacity, expert_in, expert_out, shared_in, shared_out, route_gate, shared_gate
):
    experts = lax.axis_size("ep")
    chips = experts // 2
    count, width = tokens.shape
    tasks = shared_gate.shape[1] // width
    units = shared_in.shape[1]
    depth = max(4, 4 * count // experts)
    me = lax.axis_index("ep").astype(I32).reshape(1)
    pick = lax.axis_index("dp").astype(I32).reshape(1)

    def swap(x, mask):
        return lax.ppermute(x, "ep", [(i, i ^ mask) for i in range(experts)])

    def across(x):
        groups = lax.axis_size("dp")
        return lax.ppermute(x, "dp", [(i, groups - 1 - i) for i in range(groups)])

    half = chips // 2
    near = near_masks(chips)
    turned = routes.T
    packed, sent, limit = pack(
        me, pick, shared_in, shared_out, route_gate, tokens, turned, capacity, tasks
    )
    opposite = swap(sent, half * 2)
    partner = swap(sent, 1)
    opposite_partner = swap(opposite, 1)
    visitor = across(tokens)
    partner_visitor = swap(visitor, 1)

    shards = {0: packed}
    for q in range(1, chips):
        shards[q] = swap(shards[q & (q - 1)], 2 * (q & -q))

    *outgoing, rows = dispatch(me, limit, sent, partner, depth, 1)
    passing = dispatch(me, limit, opposite, opposite_partner, depth, 0)
    arrived = {0: outgoing[0], half: passing[0]}
    for m in near:
        arrived[m] = swap(outgoing[m], 2 * m)
        arrived[half + m] = swap(passing[m], 2 * m)

    w1, w2 = load(expert_in[0], expert_out[0])
    early, late = [0, half] + near, [half + m for m in near]
    results = dict(zip(early, expert(w1, w2, [arrived[m] for m in early])))
    results.update(zip(late, expert(w1, w2, [arrived[m] for m in late])))
    back = {0: results[0]}
    for m in early[1:] + late:
        back[m] = swap(results[m], 2 * m)

    guests, own = (visitor, partner_visitor), (sent, partner)
    low = [shards[q] for q in range(half)]
    high = [shards[q] for q in range(half, chips)]
    part = shared(low, units, guests + own, count)
    guest_keep, guest_send = shared(high, units, guests, count, part, 0)
    keep, send = shared(high, units, own, count, part, 2 * count, True)
    guest_summed = swap(guest_send, 1)
    summed = swap(send, 1)
    crossing = (guest_keep.astype(F32) + guest_summed.astype(F32)).astype(BF)
    far_rows = across(crossing)
    order = tuple(2 * q for q in range(chips))
    w = weights(me, pick, rows, sent, send, summed, shared_gate, tasks, order)
    mine, other = collect(w, [back[m] for m in range(chips)], 4 * (-(-tasks // PAD) * PAD))
    theirs = swap(other, 1)
    mixed = mix(w, mine, theirs, keep, summed, far_rows, tasks)
    return mixed.transpose(1, 0, 2)


def near_masks(chips):
    return list(range(chips // 2 - 1, 0, -1))


def solution(mesh):
    return jax.shard_map(
        on_device,
        mesh=mesh,
        in_specs=(
            P(("dp", "ep"), None),
            P(("dp", "ep"), None),
            P(),
            P("ep", None, None),
            P("ep", None, None),
            P(None, "ep", None),
            P(None, "ep", None),
            P("ep", None),
            P(),
        ),
        out_specs=P(("dp", "ep"), None, None),
        check_vma=False,
    )
```

```python
import functools

import jax
import jax.numpy as jnp
from jax import lax
from jax.experimental import pallas as pl
from jax.experimental.pallas import tpu as pltpu
from jax.sharding import PartitionSpec as P


BF, F32, I32 = jnp.bfloat16, jnp.float32, jnp.int32
GRANT = 24 << 20
PAD = 16
NAMES = 8


def whole(shape):
    return pl.BlockSpec(shape, lambda *_: (0,) * len(shape))


def call(kernel, out_shape, **kw):
    return pl.pallas_call(
        kernel,
        out_shape=out_shape,
        compiler_params=pltpu.CompilerParams(vmem_limit_bytes=GRANT),
        **kw,
    )


def in_hbm(x):
    return pltpu.with_memory_space_constraint(x, pltpu.HBM)


def cost(flops, size):
    return pl.CostEstimate(flops=int(flops), bytes_accessed=int(size), transcendentals=0)


def dot_t(a, b):
    return lax.dot_general(a, b, (((1,), (1,)), ((), ())), preferred_element_type=F32)


def pack_kernel(tasks, me_ref, pick_ref, *refs):
    (in_ref, out_ref, gate_ref, t_ref, r_ref, c_ref, packed_ref, sent_ref, limit_ref) = refs[:9]
    gates, routes, caps, sems = refs[9:]
    units, width = in_ref.shape[1:]
    count = t_ref.shape[0]
    pick, me = pick_ref[0], me_ref[0]
    copies = [
        pltpu.make_async_copy(source, target, sems.at[i])
        for i, (source, target) in enumerate(
            (
                (r_ref, routes),
                (c_ref, caps),
                (gate_ref, gates),
                (t_ref, sent_ref.at[0:count]),
                (in_ref.at[pick], packed_ref.at[0:units]),
                (out_ref.at[pick], packed_ref.at[units : 2 * units]),
            )
        )
    ]
    for copy in copies:
        copy.start()
    for copy in copies[:3]:
        copy.wait()
    blank = jnp.zeros((NAMES - routes.shape[0], count), F32)
    named = jnp.concatenate([routes[...].astype(F32), blank], axis=0).astype(BF)
    sent_ref[count:] = jnp.concatenate([named, jnp.zeros((NAMES, width - count), BF)], axis=1)
    rows = [gates[:, s * width : (s + 1) * width] for s in range(tasks)]
    rows.append(jnp.zeros((packed_ref.shape[0] - 2 * units - tasks, width), BF))
    packed_ref[2 * units :] = jnp.concatenate(rows, axis=0)
    ids = lax.broadcasted_iota(I32, limit_ref.shape, 0)
    limit = jnp.zeros(limit_ref.shape, F32)
    for q in range(limit_ref.shape[0]):
        limit = jnp.where(ids == q, caps[q ^ me].astype(F32), limit)
    limit_ref[...] = limit
    for copy in copies[3:]:
        copy.wait()


def pack(me, pick, shared_in, shared_out, route_gate, tokens, routes, capacity, tasks):
    _, units, width = shared_in.shape
    count = tokens.shape[0]
    rows = 2 * units + -(-tasks // PAD) * PAD
    smem = pl.BlockSpec(memory_space=pltpu.SMEM)
    vmem = pl.BlockSpec(memory_space=pltpu.VMEM)
    return call(
        functools.partial(pack_kernel, tasks),
        [
            jax.ShapeDtypeStruct((rows, width), BF),
            jax.ShapeDtypeStruct((count + NAMES, width), BF),
            jax.ShapeDtypeStruct((capacity.shape[0], count), F32),
        ],
        in_specs=[smem, smem] + [pl.BlockSpec(memory_space=pltpu.HBM)] * 6,
        out_specs=[vmem] * 3,
        scratch_shapes=[
            pltpu.VMEM(route_gate.shape, BF),
            pltpu.VMEM(routes.shape, I32),
            pltpu.SMEM(capacity.shape, I32),
            pltpu.SemaphoreType.DMA((6,)),
        ],
    )(me, pick, *map(in_hbm, (shared_in, shared_out, route_gate, tokens, routes, capacity)))


def dispatch_kernel(targets, depth, me_ref, limit_ref, t0_ref, t1_ref, *outs):
    me = me_ref[0]
    experts, count = limit_ref.shape
    ids = lax.broadcasted_iota(I32, (experts, count), 0)
    earlier = lax.broadcasted_iota(I32, (count, count), 0) < lax.broadcasted_iota(
        I32, (count, count), 1
    )
    upper = jnp.where(earlier, 1.0, 0.0).astype(BF)
    slot = lax.broadcasted_iota(I32, (depth, count), 0).astype(F32)
    for side, sent in enumerate((t0_ref, t1_ref)):
        rel = routes_of(sent, count) ^ me
        named = [rel[k : k + 1] == ids for k in range(2)]
        chosen = jnp.logical_or(*named)
        before = jnp.dot(jnp.where(chosen, 1.0, 0.0).astype(BF), upper, preferred_element_type=F32)
        kept = jnp.logical_and(chosen, before < limit_ref[...])
        ranked = jnp.where(kept, before, -1.0)
        table = jnp.concatenate(
            [
                jnp.where(ranked[2 * m : 2 * m + 1] == slot, 1.0, 0.0).astype(BF)
                for m in range(targets)
            ],
            axis=0,
        )
        picked = jnp.dot(table, sent[0:count], preferred_element_type=F32).astype(BF)
        for m in range(targets):
            outs[m][side * depth : (side + 1) * depth] = picked[m * depth : (m + 1) * depth]
        if side == 0 and len(outs) > targets:
            keeps, codes = [], []
            for k, here in enumerate(named):
                rank = jnp.sum(jnp.where(here, ranked, 0.0), axis=0, keepdims=True)
                keep = rank >= 0.0
                place = ((rel[k : k + 1] >> 1) * depth).astype(F32) + rank
                even = (rel[k : k + 1] & 1) == 0
                keeps.append(jnp.where(keep, 1.0, 0.0))
                for parity in (even, jnp.logical_not(even)):
                    codes.append(jnp.where(jnp.logical_and(keep, parity), place, -1.0))
            blank = jnp.zeros((8 - len(codes) - len(keeps), count), F32)
            outs[targets][...] = jnp.concatenate(codes + keeps + [blank], axis=0)


def routes_of(sent, count):
    return sent[count:, 0:count].astype(F32)[0:2].astype(I32)


def dispatch(me, limit, t0, t1, depth, slots):
    targets = limit.shape[0] // 4
    count, width = limit.shape[1], t0.shape[1]
    smem = pl.BlockSpec(memory_space=pltpu.SMEM)
    vmem = pl.BlockSpec(memory_space=pltpu.VMEM)
    return call(
        functools.partial(dispatch_kernel, targets, depth),
        [jax.ShapeDtypeStruct((2 * depth, width), BF)] * targets
        + [jax.ShapeDtypeStruct((8, count), F32)] * slots,
        in_specs=[smem] + [vmem] * 3,
        out_specs=[vmem] * (targets + slots),
        cost_estimate=cost(4 * targets * depth * count * width, 6 * count * width),
    )(me, limit, t0, t1)


def load_kernel(a_ref, b_ref, a_out, b_out, sems):
    parts = sems.shape[1]
    copies = []
    for j, (source, target) in enumerate(((a_ref, a_out), (b_ref, b_out))):
        rows = source.shape[0] // parts
        for i in range(parts):
            piece = pl.ds(i * rows, rows)
            copies.append(
                pltpu.make_async_copy(source.at[piece], target.at[piece], sems.at[j, i])
            )
    for copy in copies:
        copy.start()
    for copy in copies:
        copy.wait()


def load(a, b):
    return call(
        load_kernel,
        [jax.ShapeDtypeStruct(a.shape, a.dtype), jax.ShapeDtypeStruct(b.shape, b.dtype)],
        in_specs=[pl.BlockSpec(memory_space=pltpu.HBM)] * 2,
        out_specs=[pl.BlockSpec(memory_space=pltpu.VMEM)] * 2,
        scratch_shapes=[pltpu.SemaphoreType.DMA((2, 4))],
        cost_estimate=cost(0, 4 * (a.size + b.size)),
    )(in_hbm(a), in_hbm(b))


def expert_kernel(blocks, w1_ref, w2_ref, *refs):
    ins, outs, x_ref, acc_ref = refs[:blocks], refs[blocks : 2 * blocks], refs[-2], refs[-1]
    step = pl.program_id(0)
    rows = ins[0].shape[0]

    @pl.when(step == 0)
    def _():
        for i in range(blocks):
            x_ref[i * rows : (i + 1) * rows] = ins[i][...]

    hidden = jax.nn.gelu(jnp.dot(x_ref[...], w1_ref[...], preferred_element_type=F32)).astype(BF)
    part = jnp.dot(hidden, w2_ref[...], preferred_element_type=F32)

    @pl.when(step == 0)
    def _():
        acc_ref[...] = part

    @pl.when(step > 0)
    def _():
        acc_ref[...] += part

    @pl.when(step == pl.num_programs(0) - 1)
    def _():
        for i in range(blocks):
            outs[i][...] = acc_ref[i * rows : (i + 1) * rows].astype(BF)


def expert(w1, w2, xs, tile=1024):
    width, units = w1.shape
    tile = min(tile, units)
    rows = xs[0].shape[0]
    total = rows * len(xs)
    row_spec = whole((rows, width))
    return call(
        functools.partial(expert_kernel, len(xs)),
        [jax.ShapeDtypeStruct((rows, width), BF)] * len(xs),
        grid=(units // tile,),
        in_specs=[
            pl.BlockSpec((width, tile), lambda i: (0, i)),
            pl.BlockSpec((tile, width), lambda i: (i, 0)),
        ]
        + [row_spec] * len(xs),
        out_specs=[row_spec] * len(xs),
        scratch_shapes=[pltpu.VMEM((total, width), BF), pltpu.VMEM((total, width), F32)],
        cost_estimate=cost(4 * total * width * units, 4 * width * (units + total)),
    )(w1, w2, *xs)


def shared_kernel(shards, units, group, start, gated, count, *refs):
    ins, refs = refs[:shards], refs[shards:]
    x_ref = refs[-1]
    blocks = x_ref.shape[0] // count
    for i in range(blocks):
        x_ref[i * count : (i + 1) * count] = refs[i][0:count]
    refs = refs[blocks:-1]
    total = None
    for first in range(0, shards, group):
        part = ins[first : first + group]
        up = jnp.concatenate([w[0:units] for w in part], axis=0)
        down = jnp.concatenate([w[units : 2 * units] for w in part], axis=0)
        hidden = jax.nn.gelu(dot_t(x_ref[...], up)).astype(BF)
        term = jnp.dot(hidden, down, preferred_element_type=F32)
        total = term if total is None else total + term
    if start is None:
        refs[0][...] = total
        refs[1][...] = jnp.concatenate([w[2 * units :] for w in ins], axis=0)
        return
    before, early, keep_ref, send_ref = refs
    total = total + before[start : start + blocks * count]
    keep_ref[...] = total[0:count].astype(BF)
    send_ref[0:count] = total[count:].astype(BF)
    if gated:
        gates = jnp.concatenate([early[...]] + [w[2 * units :] for w in ins], axis=0)
        send_ref[count:] = gates


def shared(shards, units, tokens, count, carried=(), start=None, gated=False):
    width = shards[0].shape[1]
    gates = len(shards) * (shards[0].shape[0] - 2 * units)
    vmem = pl.BlockSpec(memory_space=pltpu.VMEM)
    if carried:
        extra = 2 * gates if gated else 0
        shapes = [((count, width), BF), ((count + extra, width), BF)]
    else:
        shapes = [((len(tokens) * count, width), F32), ((gates, width), BF)]
    group = max(1, min(len(shards), 256 // units))
    return call(
        functools.partial(shared_kernel, len(shards), units, group, start, gated, count),
        [jax.ShapeDtypeStruct(*shape) for shape in shapes],
        in_specs=[vmem] * (len(shards) + len(tokens) + len(carried)),
        out_specs=[vmem] * 2,
        scratch_shapes=[pltpu.VMEM((len(tokens) * count, width), BF)],
        cost_estimate=cost(
            4 * len(tokens) * count * width * units * len(shards), 4 * len(shards) * units * width
        ),
    )(*shards, *tokens, *carried)


def weight_kernel(tasks, order, me_ref, pick_ref, rows_ref, t_ref, g0_ref, g1_ref, s_ref, w_ref):
    count = rows_ref.shape[1]
    width = t_ref.shape[1]
    me, pick = me_ref[0], pick_ref[0]
    rel = routes_of(t_ref, count) ^ me
    tokens = t_ref[0:count]
    gates = -(-tasks // PAD) * PAD
    total = len(order) * gates

    def logits(g):
        return dot_t(g, tokens).astype(BF).astype(F32)

    chosen = [jnp.zeros((gates, count), F32) for _ in range(2)]
    for parity, ref in ((0, g0_ref), (1, g1_ref)):
        found = logits(ref[ref.shape[0] - total :])
        for p, q in enumerate(order):
            for k in range(2):
                chosen[k] = jnp.where(
                    rel[k : k + 1] == q ^ parity, found[p * gates : (p + 1) * gates], chosen[k]
                )
    values = [rows_ref[4 + k : 5 + k] * jax.nn.sigmoid(chosen[k]) for k in range(2)]
    own = []
    for j in range(2):
        gate = jnp.concatenate(
            [s_ref[j : j + 1, s * width : (s + 1) * width] for s in range(tasks)]
            + [jnp.zeros((gates - tasks, width), BF)],
            axis=0,
        )
        own.append(jax.nn.sigmoid(logits(gate)))
    total = values[0] + values[1] + own[0] + own[1]
    first = jnp.where(pick == 0, own[0], own[1])
    second = jnp.where(pick == 0, own[1], own[0])
    columns = [v / total for v in (values[0], values[1], first, second)] + [rows_ref[...]]
    high = sum(c.shape[0] for c in columns)
    full = -(-high // 128) * 128
    columns.append(jnp.zeros((full - high, count), F32))
    w_ref[...] = jnp.concatenate(columns, axis=0).T


def weights(me, pick, rows, sent, g0, g1, shared_gate, tasks, order):
    smem = pl.BlockSpec(memory_space=pltpu.SMEM)
    vmem = pl.BlockSpec(memory_space=pltpu.VMEM)
    gates = -(-tasks // PAD) * PAD
    full = -(-(4 * gates + rows.shape[0]) // 128) * 128
    return call(
        functools.partial(weight_kernel, tasks, order),
        jax.ShapeDtypeStruct((rows.shape[1], full), F32),
        in_specs=[smem, smem] + [vmem] * 5,
        out_specs=vmem,
        cost_estimate=cost(8 * sent.size * gates * len(order), 4 * g0.size + 2 * sent.size),
    )(me, pick, rows, sent, g0, g1, shared_gate)


def stack_kernel(*refs):
    depth = refs[0].shape[0] // 2
    for i, r in enumerate(refs[:-1]):
        refs[-1][i * depth : (i + 1) * depth] = r[depth:]


def stack(blocks):
    vmem = pl.BlockSpec(memory_space=pltpu.VMEM)
    rows, width = blocks[0].shape
    return call(
        stack_kernel,
        jax.ShapeDtypeStruct((len(blocks) * rows // 2, width), BF),
        in_specs=[vmem] * len(blocks),
        out_specs=vmem,
    )(*blocks)


def slots_of(masks, depth):
    lane = lax.broadcasted_iota(I32, (8, len(masks) * depth), 1)
    ids, before = lane, 0
    for i, m in enumerate(masks):
        step = m * depth - i * depth
        ids = ids + jnp.where(lane >= i * depth, step - before, 0)
        before = step
    return ids[0:1].astype(F32)


def picks(w_ref, column, ids):
    return jnp.where(w_ref[:, column : column + 1] == ids, 1.0, 0.0).astype(BF)


def collect_kernel(masks, early, first, w_ref, *refs):
    own, theirs, out = refs[: len(masks)], refs[-2], refs[-1]
    depth = own[0].shape[0] // 2
    count = w_ref.shape[0]
    rows = jnp.concatenate([r[0:depth] for r in own] + [theirs[...]], axis=0)
    own_ids, their_ids = slots_of(masks, depth), slots_of(early, depth)
    for k in range(2):
        column = first + 2 * k
        table = jnp.concatenate(
            [picks(w_ref, column, own_ids), picks(w_ref, column + 1, their_ids)], axis=1
        )
        out[k * count : (k + 1) * count] = jnp.dot(
            table, rows, preferred_element_type=F32
        ).astype(BF)


def collect(w, masks, blocks, early, theirs, first):
    vmem = pl.BlockSpec(memory_space=pltpu.VMEM)
    count, width = w.shape[0], blocks[0].shape[1]
    slots = theirs.shape[0] + sum(b.shape[0] for b in blocks) // 2
    return call(
        functools.partial(collect_kernel, masks, early, first),
        jax.ShapeDtypeStruct((2 * count, width), BF),
        in_specs=[vmem] * (2 + len(blocks)),
        out_specs=vmem,
        cost_estimate=cost(4 * count * slots * width, 2 * slots * width + 4 * count * width),
    )(w, *blocks, theirs)


def mix_kernel(tasks, gates, late, depth, block, part, w_ref, a_ref, l_ref, s0, s1, x_ref, out_ref, held, sems):
    first = 4 * gates
    count = w_ref.shape[0]
    ids = slots_of(late, depth)
    row = lax.broadcasted_iota(I32, (part, 4 * part), 0)
    lane = lax.broadcasted_iota(I32, (part, 4 * part), 1)
    here = [lane == row + j * part for j in range(4)]
    copies = []
    for low in range(0, count, block):
        span = slice(low, low + block)
        found = [
            a_ref[k * count + low : k * count + low + block]
            + jnp.dot(
                picks(w_ref.at[span], first + 2 * k + 1, ids),
                l_ref[...],
                preferred_element_type=F32,
            ).astype(BF)
            for k in range(2)
        ]
        found += [(s0[span].astype(F32) + s1[span].astype(F32)).astype(BF), x_ref[span]]
        for start in range(0, block, part):
            rows = jnp.concatenate([f[start : start + part] for f in found], axis=0)
            here_rows = slice(low + start, low + start + part)
            table = []
            for s in range(tasks):
                entry = jnp.zeros((part, 4 * part), F32)
                for j in range(4):
                    column = w_ref[here_rows, j * gates + s : j * gates + s + 1]
                    entry = jnp.where(here[j], column, entry)
                table.append(entry.astype(BF))
            mixed = jnp.dot(jnp.concatenate(table, axis=0), rows, preferred_element_type=F32)
            for s in range(tasks):
                held[s, here_rows] = mixed[s * part : (s + 1) * part].astype(BF)
            copies.append(
                pltpu.make_async_copy(
                    held.at[:, here_rows], out_ref.at[:, here_rows], sems.at[len(copies)]
                )
            )
            copies[-1].start()
    for copy in copies:
        copy.wait()


def mix(w, found, late, theirs, keep, back, far, tasks, depth, block=128, part=32):
    count = w.shape[0]
    width = far.shape[1]
    gates = -(-tasks // PAD) * PAD
    vmem = pl.BlockSpec(memory_space=pltpu.VMEM)
    return call(
        functools.partial(mix_kernel, tasks, gates, late, depth, block, part),
        jax.ShapeDtypeStruct((tasks, count, width), BF),
        in_specs=[vmem] * 6,
        out_specs=pl.BlockSpec(memory_space=pltpu.HBM),
        scratch_shapes=[
            pltpu.VMEM((tasks, count, width), BF),
            pltpu.SemaphoreType.DMA((count // part,)),
        ],
        cost_estimate=cost(8 * tasks * count * width, 2 * (tasks + 8) * count * width),
    )(w, found, theirs, keep, back, far)


def on_device(
    tokens, routes, capacity, expert_in, expert_out, shared_in, shared_out, route_gate, shared_gate
):
    experts = lax.axis_size("ep")
    chips = experts // 2
    count, width = tokens.shape
    tasks = shared_gate.shape[1] // width
    units = shared_in.shape[1]
    depth = max(4, 4 * count // experts)
    me = lax.axis_index("ep").astype(I32).reshape(1)
    pick = lax.axis_index("dp").astype(I32).reshape(1)

    def swap(x, mask):
        return lax.ppermute(x, "ep", [(i, i ^ mask) for i in range(experts)])

    def across(x):
        groups = lax.axis_size("dp")
        return lax.ppermute(x, "dp", [(i, groups - 1 - i) for i in range(groups)])

    half = chips // 2
    near = near_masks(chips)
    turned = routes.T
    packed, sent, limit = pack(
        me, pick, shared_in, shared_out, route_gate, tokens, turned, capacity, tasks
    )
    opposite = swap(sent, half * 2)
    partner = swap(sent, 1)
    opposite_partner = swap(opposite, 1)
    visitor = across(tokens)
    partner_visitor = swap(visitor, 1)

    shards = {0: packed}
    for q in range(1, chips):
        shards[q] = swap(shards[q & (q - 1)], 2 * (q & -q))

    *outgoing, rows = dispatch(me, limit, sent, partner, depth, 1)
    passing = dispatch(me, limit, opposite, opposite_partner, depth, 0)
    arrived = {0: outgoing[0], half: passing[0]}
    for m in near:
        arrived[m] = swap(outgoing[m], 2 * m)
        arrived[half + m] = swap(passing[m], 2 * m)

    w1, w2 = load(expert_in[0], expert_out[0])
    early, late = [0, half] + near, [half + m for m in near]
    results = dict(zip(early, expert(w1, w2, [arrived[m] for m in early])))
    results.update(zip(late, expert(w1, w2, [arrived[m] for m in late])))
    back = {0: results[0]}
    for m in early[1:] + late:
        back[m] = swap(results[m], 2 * m)

    guests, own = (visitor, partner_visitor), (sent, partner)
    low = [shards[q] for q in range(half)]
    high = [shards[q] for q in range(half, chips)]
    part = shared(low, units, guests + own, count)
    guest_keep, guest_send = shared(high, units, guests, count, part, 0)
    keep, send = shared(high, units, own, count, part, 2 * count, True)
    guest_summed = swap(guest_send, 1)
    summed = swap(send, 1)
    crossing = (guest_keep.astype(F32) + guest_summed.astype(F32)).astype(BF)
    far_rows = across(crossing)
    order = tuple(2 * q for q in range(chips))
    w = weights(me, pick, rows, sent, send, summed, shared_gate, tasks, order)
    first, last = halves(chips)
    theirs_first = swap(stack([back[m] for m in first]), 1)
    theirs_last = swap(stack([back[m] for m in last]), 1)
    masks = list(range(chips))
    found = collect(
        w, masks, [back[m] for m in masks], first, theirs_first, 4 * (-(-tasks // PAD) * PAD)
    )
    mixed = mix(w, found, last, theirs_last, keep, summed, far_rows, tasks, depth)
    return mixed.transpose(1, 0, 2)


def halves(chips):
    order = [0] + return_order(chips)
    return order[: chips // 2], order[chips // 2 :]


def return_order(chips):
    half, near = chips // 2, near_masks(chips)
    ordered = [m for m in near if m % 2 == 0] + [m for m in near if m % 2]
    return [half, 1] + [half + m for m in ordered] + [m for m in ordered if m != 1]


def near_masks(chips):
    return list(range(chips // 2 - 1, 0, -1))


def solution(mesh):
    return jax.shard_map(
        on_device,
        mesh=mesh,
        in_specs=(
            P(("dp", "ep"), None),
            P(("dp", "ep"), None),
            P(),
            P("ep", None, None),
            P("ep", None, None),
            P(None, "ep", None),
            P(None, "ep", None),
            P("ep", None),
            P(),
        ),
        out_specs=P(("dp", "ep"), None, None),
        check_vma=False,
    )
```

```python
import functools

import jax
import jax.numpy as jnp
from jax import lax
from jax.experimental import pallas as pl
from jax.experimental.pallas import tpu as pltpu
from jax.sharding import PartitionSpec as P


BF, F32, I32 = jnp.bfloat16, jnp.float32, jnp.int32
GRANT = 24 << 20
PAD = 16
NAMES = 8


def whole(shape):
    return pl.BlockSpec(shape, lambda *_: (0,) * len(shape))


def call(kernel, out_shape, **kw):
    return pl.pallas_call(
        kernel,
        out_shape=out_shape,
        compiler_params=pltpu.CompilerParams(vmem_limit_bytes=GRANT),
        **kw,
    )


def in_hbm(x):
    return pltpu.with_memory_space_constraint(x, pltpu.HBM)


def cost(flops, size):
    return pl.CostEstimate(flops=int(flops), bytes_accessed=int(size), transcendentals=0)


def dot_t(a, b):
    return lax.dot_general(a, b, (((1,), (1,)), ((), ())), preferred_element_type=F32)


def pack_kernel(tasks, me_ref, pick_ref, *refs):
    (in_ref, out_ref, gate_ref, t_ref, r_ref, c_ref, packed_ref, sent_ref, limit_ref) = refs[:9]
    gates, routes, caps, sems = refs[9:]
    units, width = in_ref.shape[1:]
    count = t_ref.shape[0]
    pick, me = pick_ref[0], me_ref[0]
    copies = [
        pltpu.make_async_copy(source, target, sems.at[i])
        for i, (source, target) in enumerate(
            (
                (r_ref, routes),
                (c_ref, caps),
                (gate_ref, gates),
                (t_ref, sent_ref.at[0:count]),
                (in_ref.at[pick], packed_ref.at[0:units]),
                (out_ref.at[pick], packed_ref.at[units : 2 * units]),
            )
        )
    ]
    for copy in copies:
        copy.start()
    for copy in copies[:3]:
        copy.wait()
    blank = jnp.zeros((NAMES - routes.shape[0], count), F32)
    named = jnp.concatenate([routes[...].astype(F32), blank], axis=0).astype(BF)
    sent_ref[count:] = jnp.concatenate([named, jnp.zeros((NAMES, width - count), BF)], axis=1)
    rows = [gates[:, s * width : (s + 1) * width] for s in range(tasks)]
    rows.append(jnp.zeros((packed_ref.shape[0] - 2 * units - tasks, width), BF))
    packed_ref[2 * units :] = jnp.concatenate(rows, axis=0)
    ids = lax.broadcasted_iota(I32, limit_ref.shape, 0)
    limit = jnp.zeros(limit_ref.shape, F32)
    for q in range(limit_ref.shape[0]):
        limit = jnp.where(ids == q, caps[q ^ me].astype(F32), limit)
    limit_ref[...] = limit
    for copy in copies[3:]:
        copy.wait()


def pack(me, pick, shared_in, shared_out, route_gate, tokens, routes, capacity, tasks):
    _, units, width = shared_in.shape
    count = tokens.shape[0]
    rows = 2 * units + -(-tasks // PAD) * PAD
    smem = pl.BlockSpec(memory_space=pltpu.SMEM)
    vmem = pl.BlockSpec(memory_space=pltpu.VMEM)
    return call(
        functools.partial(pack_kernel, tasks),
        [
            jax.ShapeDtypeStruct((rows, width), BF),
            jax.ShapeDtypeStruct((count + NAMES, width), BF),
            jax.ShapeDtypeStruct((capacity.shape[0], count), F32),
        ],
        in_specs=[smem, smem] + [pl.BlockSpec(memory_space=pltpu.HBM)] * 6,
        out_specs=[vmem] * 3,
        scratch_shapes=[
            pltpu.VMEM(route_gate.shape, BF),
            pltpu.VMEM(routes.shape, I32),
            pltpu.SMEM(capacity.shape, I32),
            pltpu.SemaphoreType.DMA((6,)),
        ],
    )(me, pick, *map(in_hbm, (shared_in, shared_out, route_gate, tokens, routes, capacity)))


def dispatch_kernel(targets, depth, me_ref, limit_ref, t0_ref, t1_ref, *outs):
    me = me_ref[0]
    experts, count = limit_ref.shape
    ids = lax.broadcasted_iota(I32, (experts, count), 0)
    earlier = lax.broadcasted_iota(I32, (count, count), 0) < lax.broadcasted_iota(
        I32, (count, count), 1
    )
    upper = jnp.where(earlier, 1.0, 0.0).astype(BF)
    slot = lax.broadcasted_iota(I32, (depth, count), 0).astype(F32)
    for side, sent in enumerate((t0_ref, t1_ref)):
        rel = routes_of(sent, count) ^ me
        named = [rel[k : k + 1] == ids for k in range(2)]
        chosen = jnp.logical_or(*named)
        before = jnp.dot(jnp.where(chosen, 1.0, 0.0).astype(BF), upper, preferred_element_type=F32)
        kept = jnp.logical_and(chosen, before < limit_ref[...])
        ranked = jnp.where(kept, before, -1.0)
        table = jnp.concatenate(
            [
                jnp.where(ranked[2 * m : 2 * m + 1] == slot, 1.0, 0.0).astype(BF)
                for m in range(targets)
            ],
            axis=0,
        )
        picked = jnp.dot(table, sent[0:count], preferred_element_type=F32).astype(BF)
        for m in range(targets):
            outs[m][side * depth : (side + 1) * depth] = picked[m * depth : (m + 1) * depth]
        if side == 0 and len(outs) > targets:
            keeps, codes = [], []
            for k, here in enumerate(named):
                rank = jnp.sum(jnp.where(here, ranked, 0.0), axis=0, keepdims=True)
                keep = rank >= 0.0
                place = ((rel[k : k + 1] >> 1) * depth).astype(F32) + rank
                even = (rel[k : k + 1] & 1) == 0
                keeps.append(jnp.where(keep, 1.0, 0.0))
                for parity in (even, jnp.logical_not(even)):
                    codes.append(jnp.where(jnp.logical_and(keep, parity), place, -1.0))
            blank = jnp.zeros((8 - len(codes) - len(keeps), count), F32)
            outs[targets][...] = jnp.concatenate(codes + keeps + [blank], axis=0)


def routes_of(sent, count):
    return sent[count:, 0:count].astype(F32)[0:2].astype(I32)


def dispatch(me, limit, t0, t1, depth, slots):
    targets = limit.shape[0] // 4
    count, width = limit.shape[1], t0.shape[1]
    smem = pl.BlockSpec(memory_space=pltpu.SMEM)
    vmem = pl.BlockSpec(memory_space=pltpu.VMEM)
    return call(
        functools.partial(dispatch_kernel, targets, depth),
        [jax.ShapeDtypeStruct((2 * depth, width), BF)] * targets
        + [jax.ShapeDtypeStruct((8, count), F32)] * slots,
        in_specs=[smem] + [vmem] * 3,
        out_specs=[vmem] * (targets + slots),
        cost_estimate=cost(4 * targets * depth * count * width, 6 * count * width),
    )(me, limit, t0, t1)


def load_kernel(a_ref, b_ref, a_out, b_out, sems):
    parts = sems.shape[1]
    copies = []
    for j, (source, target) in enumerate(((a_ref, a_out), (b_ref, b_out))):
        rows = source.shape[0] // parts
        for i in range(parts):
            piece = pl.ds(i * rows, rows)
            copies.append(
                pltpu.make_async_copy(source.at[piece], target.at[piece], sems.at[j, i])
            )
    for copy in copies:
        copy.start()
    for copy in copies:
        copy.wait()


def load(a, b):
    return call(
        load_kernel,
        [jax.ShapeDtypeStruct(a.shape, a.dtype), jax.ShapeDtypeStruct(b.shape, b.dtype)],
        in_specs=[pl.BlockSpec(memory_space=pltpu.HBM)] * 2,
        out_specs=[pl.BlockSpec(memory_space=pltpu.VMEM)] * 2,
        scratch_shapes=[pltpu.SemaphoreType.DMA((2, 4))],
        cost_estimate=cost(0, 4 * (a.size + b.size)),
    )(in_hbm(a), in_hbm(b))


def expert_kernel(blocks, w1_ref, w2_ref, *refs):
    ins, outs, x_ref, acc_ref = refs[:blocks], refs[blocks : 2 * blocks], refs[-2], refs[-1]
    step = pl.program_id(0)
    rows = ins[0].shape[0]

    @pl.when(step == 0)
    def _():
        for i in range(blocks):
            x_ref[i * rows : (i + 1) * rows] = ins[i][...]

    hidden = jax.nn.gelu(jnp.dot(x_ref[...], w1_ref[...], preferred_element_type=F32)).astype(BF)
    part = jnp.dot(hidden, w2_ref[...], preferred_element_type=F32)

    @pl.when(step == 0)
    def _():
        acc_ref[...] = part

    @pl.when(step > 0)
    def _():
        acc_ref[...] += part

    @pl.when(step == pl.num_programs(0) - 1)
    def _():
        for i in range(blocks):
            outs[i][...] = acc_ref[i * rows : (i + 1) * rows].astype(BF)


def expert(w1, w2, xs, tile=1024):
    width, units = w1.shape
    tile = min(tile, units)
    rows = xs[0].shape[0]
    total = rows * len(xs)
    row_spec = whole((rows, width))
    return call(
        functools.partial(expert_kernel, len(xs)),
        [jax.ShapeDtypeStruct((rows, width), BF)] * len(xs),
        grid=(units // tile,),
        in_specs=[
            pl.BlockSpec((width, tile), lambda i: (0, i)),
            pl.BlockSpec((tile, width), lambda i: (i, 0)),
        ]
        + [row_spec] * len(xs),
        out_specs=[row_spec] * len(xs),
        scratch_shapes=[pltpu.VMEM((total, width), BF), pltpu.VMEM((total, width), F32)],
        cost_estimate=cost(4 * total * width * units, 4 * width * (units + total)),
    )(w1, w2, *xs)


def shared_kernel(shards, units, group, start, gated, count, *refs):
    ins, refs = refs[:shards], refs[shards:]
    x_ref = refs[-1]
    blocks = x_ref.shape[0] // count
    for i in range(blocks):
        x_ref[i * count : (i + 1) * count] = refs[i][0:count]
    refs = refs[blocks:-1]
    total = None
    for first in range(0, shards, group):
        part = ins[first : first + group]
        up = jnp.concatenate([w[0:units] for w in part], axis=0)
        down = jnp.concatenate([w[units : 2 * units] for w in part], axis=0)
        hidden = jax.nn.gelu(dot_t(x_ref[...], up)).astype(BF)
        term = jnp.dot(hidden, down, preferred_element_type=F32)
        total = term if total is None else total + term
    if start is None:
        refs[0][...] = total
        refs[1][...] = jnp.concatenate([w[2 * units :] for w in ins], axis=0)
        return
    before, early, keep_ref, send_ref = refs
    total = total + before[start : start + blocks * count]
    keep_ref[...] = total[0:count].astype(BF)
    send_ref[0:count] = total[count:].astype(BF)
    if gated:
        gates = jnp.concatenate([early[...]] + [w[2 * units :] for w in ins], axis=0)
        send_ref[count:] = gates


def shared(shards, units, tokens, count, carried=(), start=None, gated=False):
    width = shards[0].shape[1]
    gates = len(shards) * (shards[0].shape[0] - 2 * units)
    vmem = pl.BlockSpec(memory_space=pltpu.VMEM)
    if carried:
        extra = 2 * gates if gated else 0
        shapes = [((count, width), BF), ((count + extra, width), BF)]
    else:
        shapes = [((len(tokens) * count, width), F32), ((gates, width), BF)]
    group = max(1, min(len(shards), 256 // units))
    return call(
        functools.partial(shared_kernel, len(shards), units, group, start, gated, count),
        [jax.ShapeDtypeStruct(*shape) for shape in shapes],
        in_specs=[vmem] * (len(shards) + len(tokens) + len(carried)),
        out_specs=[vmem] * 2,
        scratch_shapes=[pltpu.VMEM((len(tokens) * count, width), BF)],
        cost_estimate=cost(
            4 * len(tokens) * count * width * units * len(shards), 4 * len(shards) * units * width
        ),
    )(*shards, *tokens, *carried)


def weight_kernel(tasks, order, me_ref, pick_ref, rows_ref, t_ref, g0_ref, g1_ref, s_ref, w_ref):
    count = rows_ref.shape[1]
    width = t_ref.shape[1]
    me, pick = me_ref[0], pick_ref[0]
    rel = routes_of(t_ref, count) ^ me
    tokens = t_ref[0:count]
    gates = -(-tasks // PAD) * PAD
    total = len(order) * gates

    def logits(g):
        return dot_t(g, tokens).astype(BF).astype(F32)

    chosen = [jnp.zeros((gates, count), F32) for _ in range(2)]
    for parity, ref in ((0, g0_ref), (1, g1_ref)):
        found = logits(ref[ref.shape[0] - total :])
        for p, q in enumerate(order):
            for k in range(2):
                chosen[k] = jnp.where(
                    rel[k : k + 1] == q ^ parity, found[p * gates : (p + 1) * gates], chosen[k]
                )
    values = [rows_ref[4 + k : 5 + k] * jax.nn.sigmoid(chosen[k]) for k in range(2)]
    own = []
    for j in range(2):
        gate = jnp.concatenate(
            [s_ref[j : j + 1, s * width : (s + 1) * width] for s in range(tasks)]
            + [jnp.zeros((gates - tasks, width), BF)],
            axis=0,
        )
        own.append(jax.nn.sigmoid(logits(gate)))
    total = values[0] + values[1] + own[0] + own[1]
    first = jnp.where(pick == 0, own[0], own[1])
    second = jnp.where(pick == 0, own[1], own[0])
    columns = [v / total for v in (values[0], values[1], first, second)] + [rows_ref[...]]
    high = sum(c.shape[0] for c in columns)
    full = -(-high // 128) * 128
    columns.append(jnp.zeros((full - high, count), F32))
    w_ref[...] = jnp.concatenate(columns, axis=0).T


def weights(me, pick, rows, sent, g0, g1, shared_gate, tasks, order):
    smem = pl.BlockSpec(memory_space=pltpu.SMEM)
    vmem = pl.BlockSpec(memory_space=pltpu.VMEM)
    gates = -(-tasks // PAD) * PAD
    full = -(-(4 * gates + rows.shape[0]) // 128) * 128
    return call(
        functools.partial(weight_kernel, tasks, order),
        jax.ShapeDtypeStruct((rows.shape[1], full), F32),
        in_specs=[smem, smem] + [vmem] * 5,
        out_specs=vmem,
        cost_estimate=cost(8 * sent.size * gates * len(order), 4 * g0.size + 2 * sent.size),
    )(me, pick, rows, sent, g0, g1, shared_gate)


def stack_kernel(*refs):
    depth = refs[0].shape[0] // 2
    for i, r in enumerate(refs[:-1]):
        refs[-1][i * depth : (i + 1) * depth] = r[depth:]


def stack(blocks):
    vmem = pl.BlockSpec(memory_space=pltpu.VMEM)
    rows, width = blocks[0].shape
    return call(
        stack_kernel,
        jax.ShapeDtypeStruct((len(blocks) * rows // 2, width), BF),
        in_specs=[vmem] * len(blocks),
        out_specs=vmem,
    )(*blocks)


def slots_of(masks, depth):
    lane = lax.broadcasted_iota(I32, (8, len(masks) * depth), 1)
    ids, before = lane, 0
    for i, m in enumerate(masks):
        step = m * depth - i * depth
        ids = ids + jnp.where(lane >= i * depth, step - before, 0)
        before = step
    return ids[0:1].astype(F32)


def picks(w_ref, column, ids):
    return jnp.where(w_ref[:, column : column + 1] == ids, 1.0, 0.0).astype(BF)


def collect_kernel(masks, early, first, w_ref, *refs):
    own, theirs, out = refs[: len(masks)], refs[-2], refs[-1]
    depth = own[0].shape[0] // 2
    count = w_ref.shape[0]
    rows = jnp.concatenate([r[0:depth] for r in own] + [theirs[...]], axis=0)
    own_ids, their_ids = slots_of(masks, depth), slots_of(early, depth)
    for k in range(2):
        column = first + 2 * k
        table = jnp.concatenate(
            [picks(w_ref, column, own_ids), picks(w_ref, column + 1, their_ids)], axis=1
        )
        out[k * count : (k + 1) * count] = jnp.dot(
            table, rows, preferred_element_type=F32
        ).astype(BF)


def collect(w, masks, blocks, early, theirs, first):
    vmem = pl.BlockSpec(memory_space=pltpu.VMEM)
    count, width = w.shape[0], blocks[0].shape[1]
    slots = theirs.shape[0] + sum(b.shape[0] for b in blocks) // 2
    return call(
        functools.partial(collect_kernel, masks, early, first),
        jax.ShapeDtypeStruct((2 * count, width), BF),
        in_specs=[vmem] * (2 + len(blocks)),
        out_specs=vmem,
        cost_estimate=cost(4 * count * slots * width, 2 * slots * width + 4 * count * width),
    )(w, *blocks, theirs)


def table_kernel(tasks, gates, part, w_ref, m_ref):
    row = lax.broadcasted_iota(I32, (part, 4 * part), 0)
    lane = lax.broadcasted_iota(I32, (part, 4 * part), 1)
    here = [lane == row + j * part for j in range(4)]
    for start in range(0, w_ref.shape[0], part):
        for s in range(tasks):
            entry = jnp.zeros((part, 4 * part), F32)
            for j in range(4):
                column = w_ref[start : start + part, j * gates + s : j * gates + s + 1]
                entry = jnp.where(here[j], column, entry)
            place = start * tasks + s * part
            m_ref[place : place + part] = entry.astype(BF)


def table(w, tasks, part=32):
    vmem = pl.BlockSpec(memory_space=pltpu.VMEM)
    return call(
        functools.partial(table_kernel, tasks, -(-tasks // PAD) * PAD, part),
        jax.ShapeDtypeStruct((w.shape[0] * tasks, 4 * part), BF),
        in_specs=[vmem],
        out_specs=vmem,
    )(w)


def mix_kernel(tasks, gates, late, depth, block, part, w_ref, m_ref, a_ref, l_ref, s0, s1, x_ref, out_ref, held, sems):
    first = 4 * gates
    count = w_ref.shape[0]
    ids = slots_of(late, depth)
    copies = []
    for low in range(0, count, block):
        span = slice(low, low + block)
        found = [
            a_ref[k * count + low : k * count + low + block]
            + jnp.dot(
                picks(w_ref.at[span], first + 2 * k + 1, ids),
                l_ref[...],
                preferred_element_type=F32,
            ).astype(BF)
            for k in range(2)
        ]
        found += [(s0[span].astype(F32) + s1[span].astype(F32)).astype(BF), x_ref[span]]
        for start in range(0, block, part):
            rows = jnp.concatenate([f[start : start + part] for f in found], axis=0)
            here_rows = slice(low + start, low + start + part)
            size = tasks * part
            table = m_ref[len(copies) * size : (len(copies) + 1) * size]
            mixed = jnp.dot(table, rows, preferred_element_type=F32)
            for s in range(tasks):
                held[s, here_rows] = mixed[s * part : (s + 1) * part].astype(BF)
            copies.append(
                pltpu.make_async_copy(
                    held.at[:, here_rows], out_ref.at[:, here_rows], sems.at[len(copies)]
                )
            )
            copies[-1].start()
    for copy in copies:
        copy.wait()


def mix(w, spread, found, late, theirs, keep, back, far, tasks, depth, block=128, part=32):
    count = w.shape[0]
    width = far.shape[1]
    gates = -(-tasks // PAD) * PAD
    vmem = pl.BlockSpec(memory_space=pltpu.VMEM)
    return call(
        functools.partial(mix_kernel, tasks, gates, late, depth, block, part),
        jax.ShapeDtypeStruct((tasks, count, width), BF),
        in_specs=[vmem] * 7,
        out_specs=pl.BlockSpec(memory_space=pltpu.HBM),
        scratch_shapes=[
            pltpu.VMEM((tasks, count, width), BF),
            pltpu.SemaphoreType.DMA((count // part,)),
        ],
        cost_estimate=cost(8 * tasks * count * width, 2 * (tasks + 8) * count * width),
    )(w, spread, found, theirs, keep, back, far)


def on_device(
    tokens, routes, capacity, expert_in, expert_out, shared_in, shared_out, route_gate, shared_gate
):
    experts = lax.axis_size("ep")
    chips = experts // 2
    count, width = tokens.shape
    tasks = shared_gate.shape[1] // width
    units = shared_in.shape[1]
    depth = max(4, 4 * count // experts)
    me = lax.axis_index("ep").astype(I32).reshape(1)
    pick = lax.axis_index("dp").astype(I32).reshape(1)

    def swap(x, mask):
        return lax.ppermute(x, "ep", [(i, i ^ mask) for i in range(experts)])

    def across(x):
        groups = lax.axis_size("dp")
        return lax.ppermute(x, "dp", [(i, groups - 1 - i) for i in range(groups)])

    half = chips // 2
    near = near_masks(chips)
    turned = routes.T
    packed, sent, limit = pack(
        me, pick, shared_in, shared_out, route_gate, tokens, turned, capacity, tasks
    )
    opposite = swap(sent, half * 2)
    partner = swap(sent, 1)
    opposite_partner = swap(opposite, 1)
    visitor = across(tokens)
    partner_visitor = swap(visitor, 1)

    shards = {0: packed}
    for q in range(1, chips):
        shards[q] = swap(shards[q & (q - 1)], 2 * (q & -q))

    *outgoing, rows = dispatch(me, limit, sent, partner, depth, 1)
    passing = dispatch(me, limit, opposite, opposite_partner, depth, 0)
    arrived = {0: outgoing[0], half: passing[0]}
    for m in near:
        arrived[m] = swap(outgoing[m], 2 * m)
        arrived[half + m] = swap(passing[m], 2 * m)

    w1, w2 = load(expert_in[0], expert_out[0])
    early, late = [0, half] + near, [half + m for m in near]
    results = dict(zip(early, expert(w1, w2, [arrived[m] for m in early])))
    results.update(zip(late, expert(w1, w2, [arrived[m] for m in late])))
    back = {0: results[0]}
    for m in early[1:] + late:
        back[m] = swap(results[m], 2 * m)

    guests, own = (visitor, partner_visitor), (sent, partner)
    low = [shards[q] for q in range(half)]
    high = [shards[q] for q in range(half, chips)]
    part = shared(low, units, guests + own, count)
    guest_keep, guest_send = shared(high, units, guests, count, part, 0)
    keep, send = shared(high, units, own, count, part, 2 * count, True)
    guest_summed = swap(guest_send, 1)
    summed = swap(send, 1)
    crossing = (guest_keep.astype(F32) + guest_summed.astype(F32)).astype(BF)
    far_rows = across(crossing)
    order = tuple(2 * q for q in range(chips))
    w = weights(me, pick, rows, sent, send, summed, shared_gate, tasks, order)
    first, last = halves(chips)
    theirs_first = swap(stack([back[m] for m in first]), 1)
    theirs_last = swap(stack([back[m] for m in last]), 1)
    masks = list(range(chips))
    found = collect(
        w, masks, [back[m] for m in masks], first, theirs_first, 4 * (-(-tasks // PAD) * PAD)
    )
    mixed = mix(w, table(w, tasks), found, last, theirs_last, keep, summed, far_rows, tasks, depth)
    return mixed.transpose(1, 0, 2)


def halves(chips):
    order = [0] + return_order(chips)
    return order[: chips // 2], order[chips // 2 :]


def return_order(chips):
    half, near = chips // 2, near_masks(chips)
    ordered = [m for m in near if m % 2 == 0] + [m for m in near if m % 2]
    return [half, 1] + [half + m for m in ordered] + [m for m in ordered if m != 1]


def near_masks(chips):
    return list(range(chips // 2 - 1, 0, -1))


def solution(mesh):
    return jax.shard_map(
        on_device,
        mesh=mesh,
        in_specs=(
            P(("dp", "ep"), None),
            P(("dp", "ep"), None),
            P(),
            P("ep", None, None),
            P("ep", None, None),
            P(None, "ep", None),
            P(None, "ep", None),
            P("ep", None),
            P(),
        ),
        out_specs=P(("dp", "ep"), None, None),
        check_vma=False,
    )
```
